128 devices in a mesh: cluster: 128 (over z, y, x, core).
Axes of the slice: x: 4, y: 4, z: 4, core: 2. Of those that a mesh axis runs over, the one named last changes fastest.
Arguments:
- charges: bfloat16 [16384, 16, 128], P('cluster'), may hold values from -6 to 6
- points: float32 [16384, 3, 128], P('cluster'), may hold values from 0 to 16384, as said below
- basis: bfloat16 [16384, 32, 128], P('cluster'), may hold values from -0.5 to 0.5
- near_list: int32 [16384, 3], P('cluster'), may hold values from -1 to 16383, as said below
- loc_coupling: bfloat16 [128, 248, 3, 1024], P('cluster'), may hold values from -0.625 to 0.625
- loc_transfer: bfloat16 [128, 248, 1024], P('cluster'), may hold values from -0.875 to 0.875
- loc_lists: int32 [128, 248, 3], P('cluster'), may hold values from -1 to 16383, as said below
- top_coupling: bfloat16 [1020, 3, 1024], replicated, may hold values from -0.625 to 0.625
- top_transfer: bfloat16 [1016, 1024], replicated, may hold values from -0.875 to 0.875
- top_lists: int32 [1020, 3], replicated, may hold values from -1 to 511, as said below
Outputs:
- potential: float32 [16384, 16, 128], P('cluster')
The draws below stay inside these ranges and needn't reach their ends.
Inputs may be any that keep to these rules, and one draw needn't show every extreme that they name: `near_list`: slot entries of leaf i are distinct; each is -1 or a leaf j with |j - i| <= 1; i itself is always listed. `loc_lists`: each entry of node c (on its level of n nodes) is -1 or a node j of that level with 2 <= |j - c| <= 3 and |floor(j / 2) - floor(c / 2)| <= 1; entries of one node are distinct. `top_lists`: as for loc_lists, on the coarse levels. `points`: component 0 of a panel of leaf i lies in [i, i + 1), the other two in [0, 1).
All inputs are finite; a program needn't handle non-finite values.
Results may differ from the reference program's by a relative error of at most 0.0029.
Values sent between devices are 32-bit elements; how exact they have to be, the bound alone decides.
No kernel may reach another device: no remote copies, remote signals or barrier semaphores. Data moves between devices by JAX's collectives and lax.ppermute only.
A program may use at most 192 MiB of HBM per device.

```python
import jax
import jax.numpy as jnp
from jax import lax

NRHS = 16
LEAF = 128
RANK = 32
KC = 3
L_DEV = 128
NLEAF = 16384
LOC_NODES = 248
TOP_NODES = 1020
N_CLUSTER = 128


def finish_lists(key, index, node_count, shift, always):
    target = index[:, None] + shift
    keep_key, order_key = jax.random.split(key)
    keeping = jax.random.randint(keep_key, target.shape, 0, 5) > 0
    keeping = (keeping | always[None, :]) & (target >= 0) & (target < node_count)
    entries = jnp.where(keeping, target, -1)
    scores = jax.random.randint(order_key, target.shape, 0, 1 << 20) * 4 + jnp.arange(3, dtype=jnp.int32)[None, :]
    order = jnp.argsort(scores, axis=1)
    return jnp.take_along_axis(entries, order, axis=1).astype(jnp.int32)


def level_lists(key, index, node_count):
    even_shift = jnp.array([-2, 2, 3], dtype=jnp.int32)
    odd_shift = jnp.array([-3, -2, 2], dtype=jnp.int32)
    shift = jnp.where((index % 2)[:, None] == 0, even_shift[None, :], odd_shift[None, :])
    return finish_lists(key, index, node_count, shift, jnp.zeros((3,), dtype=bool))


def draw_near_list(key, part):
    index = jnp.arange(NLEAF, dtype=jnp.int32)
    shift = jnp.broadcast_to(jnp.array([-1, 0, 1], dtype=jnp.int32)[None, :], (NLEAF, 3))
    always = jnp.array([False, True, False])
    return finish_lists(jax.random.fold_in(key, 11), index, NLEAF, shift, always)


def draw_loc_lists(key, part):
    pieces = []
    per_device = L_DEV
    while per_device >= 8:
        node_count = per_device * N_CLUSTER
        index = jnp.arange(node_count, dtype=jnp.int32)
        chosen = level_lists(jax.random.fold_in(key, per_device), index, node_count)
        pieces.append(chosen.reshape(N_CLUSTER, per_device, 3))
        per_device = per_device // 2
    return jnp.concatenate(pieces, axis=1)


def draw_top_lists(key, part):
    pieces = []
    node_count = 4 * N_CLUSTER
    while node_count >= 4:
        index = jnp.arange(node_count, dtype=jnp.int32)
        pieces.append(level_lists(jax.random.fold_in(key, 7000 + node_count), index, node_count))
        node_count = node_count // 2
    return jnp.concatenate(pieces, axis=0)


def draw_points(key, part):
    first_key, second_key = jax.random.split(jax.random.fold_in(key, 23))
    along = jnp.arange(NLEAF, dtype=jnp.float32)[:, None] + jax.random.uniform(first_key, (NLEAF, LEAF), jnp.float32, 0.0, 0.999)
    across = jax.random.uniform(second_key, (NLEAF, 2, LEAF), jnp.float32, 0.0, 0.999)
    return jnp.concatenate([along[:, None, :], across], axis=1).astype(jnp.float32)


def shard_levels(own_key, extent, cuts, low, largest):
    gain = 1.0
    for dim, shards_of in cuts:
        steps = jax.random.uniform(jax.random.fold_in(jax.random.fold_in(own_key, 6), dim), (shards_of,), jnp.float32, low / len(cuts), largest / len(cuts))
        gain = gain * jnp.repeat(jnp.exp(steps), extent[dim] // shards_of).reshape((-1,) + (1,) * (len(extent) - 1 - dim))
    return gain


def noise(rng, dims, scale, most, cuts=(), kind=jnp.bfloat16):
    values = jax.random.normal(rng, dims, jnp.float32) * scale
    if len(cuts) > 0:
        values = shard_levels(rng, dims, cuts, -0.22, 0.18) * values
    return jnp.clip(values, min=-most, max=most).astype(kind)


def setup_inputs(seed: int = 0) -> dict:
    keys = jax.random.split(jax.random.key(seed), 11)
    charges = noise(keys[0], (NLEAF, NRHS, LEAF), 1.0, 6.0, ((0, 128),))
    points = draw_points(jax.random.fold_in(keys[10], 71), 0)
    basis = noise(keys[2], (NLEAF, RANK, LEAF), LEAF ** -0.5, 0.5, ((0, 128),))
    near_list = draw_near_list(jax.random.fold_in(keys[10], 71), 0)
    loc_coupling = noise(keys[4], (N_CLUSTER, LOC_NODES, KC, RANK * RANK), (KC * RANK) ** -0.5, 0.625, ((0, 128),))
    loc_transfer = noise(keys[5], (N_CLUSTER, LOC_NODES, RANK * RANK), (3 * RANK // 2) ** -0.5, 0.875, ((0, 128),))
    loc_lists = draw_loc_lists(jax.random.fold_in(keys[10], 71), 0)
    top_coupling = noise(keys[7], (TOP_NODES, KC, RANK * RANK), (KC * RANK) ** -0.5, 0.625)
    top_transfer = noise(keys[8], (TOP_NODES - 4, RANK * RANK), (3 * RANK // 2) ** -0.5, 0.875)
    top_lists = draw_top_lists(jax.random.fold_in(keys[10], 71), 0)
    return {"charges": charges, "points": points, "basis": basis, "near_list": near_list, "loc_coupling": loc_coupling, "loc_transfer": loc_transfer, "loc_lists": loc_lists, "top_coupling": top_coupling, "top_transfer": top_transfer, "top_lists": top_lists}


AREA_WEIGHT = 0.0625
SOFTENING = 0.0025

def kernel_block(target, source, usable):
    displacement = target[:, None, :, :, None] - source[:, :, 0:3, None, :]
    distance_sq = lax.optimization_barrier(jnp.sum(displacement * displacement, axis=2))
    kernel = AREA_WEIGHT * lax.rsqrt(distance_sq + SOFTENING) * usable[:, :, None, None].astype(jnp.float32)
    kernel = kernel.astype(jnp.bfloat16)
    source_charges = source[:, :, 3:, :].astype(jnp.bfloat16)
    return jnp.einsum('bspq,bskq->bkp', kernel.astype(jnp.float32), source_charges.astype(jnp.float32))

def near_field(points, charges, near_list):
    leaf_count = points.shape[0]
    stacked = jnp.concatenate([points, charges.astype(jnp.float32)], axis=1)
    block_size = 16

    def apply_block(start):
        target = lax.dynamic_slice_in_dim(points, start, block_size, 0)
        chosen = lax.dynamic_slice_in_dim(near_list, start, block_size, 0)
        usable = chosen >= 0
        source = jnp.take(stacked, jnp.where(usable, chosen, 0), axis=0)
        return kernel_block(target, source, usable)
    starts = jnp.arange(0, leaf_count, block_size, dtype=jnp.int32)
    result = lax.map(apply_block, starts)
    return result.reshape(leaf_count, charges.shape[1], charges.shape[2])

def couple(window, chosen, matrices, first_node):
    node_count = chosen.shape[0]
    slots = chosen.shape[1]
    rank_width = window.shape[2]
    usable = chosen >= 0
    own_index = first_node + jnp.arange(node_count, dtype=jnp.int32)
    offset = jnp.where(usable, chosen - own_index[:, None] + 3, 3).astype(jnp.int32)
    window_index = jnp.arange(node_count, dtype=jnp.int32)[:, None] + offset
    source = jnp.take(window, window_index, axis=0) * usable[:, :, None, None].astype(jnp.float32)
    matrices = matrices.reshape(node_count, slots, rank_width, rank_width).astype(jnp.float32)
    return jnp.einsum('nskr,nsrt->nkt', source, matrices, precision=lax.Precision.HIGHEST)

def ascend(moments, lift_matrix):
    node_count, sides, rank_width = moments.shape
    matrices = lift_matrix.reshape(node_count, rank_width, rank_width).astype(jnp.float32)
    lifted = jnp.einsum('nkr,nrt->nkt', moments, matrices, precision=lax.Precision.HIGHEST)
    return lifted.reshape(node_count // 2, 2, sides, rank_width).sum(axis=1)

def descend(parent, lift_matrix, coupled):
    child_rows = jnp.repeat(parent, 2, axis=0)
    node_count, sides, rank_width = child_rows.shape
    matrices = lift_matrix.reshape(node_count, rank_width, rank_width).astype(jnp.float32)
    return coupled + jnp.einsum('nkt,nrt->nkr', child_rows, matrices, precision=lax.Precision.HIGHEST)

def reference(charges, points, basis, near_list, loc_coupling, loc_transfer, loc_lists, top_coupling, top_transfer, top_lists):
    near = near_field(points, charges, near_list)
    moments = jnp.einsum('lkp,lrp->lkr', charges.astype(jnp.float32), basis.astype(jnp.float32))
    node_count = NLEAF
    levels = []
    while node_count >= 4:
        per_device = node_count // N_CLUSTER
        lift_matrix = None
        if per_device >= 8:
            offset_node = 2 * L_DEV - 2 * per_device
            chosen = loc_lists[:, offset_node:offset_node + per_device].reshape(node_count, KC)
            matrices = loc_coupling[:, offset_node:offset_node + per_device].reshape(node_count, KC, RANK * RANK)
            lift_matrix = loc_transfer[:, offset_node:offset_node + per_device].reshape(node_count, RANK * RANK)
        else:
            offset_node = 8 * N_CLUSTER - 2 * node_count
            chosen = top_lists[offset_node:offset_node + node_count]
            matrices = top_coupling[offset_node:offset_node + node_count]
            if node_count > 4:
                lift_matrix = top_transfer[offset_node:offset_node + node_count]
        window = jnp.pad(moments, ((3, 3), (0, 0), (0, 0)))
        coupled = couple(window, chosen, matrices, 0)
        levels.append((coupled, lift_matrix))
        if node_count > 4:
            moments = ascend(moments, lift_matrix)
        node_count = node_count // 2
    expansion = levels[-1][0]
    for coupled, lift_matrix in reversed(levels[:-1]):
        expansion = descend(expansion, lift_matrix, coupled)
    leaf_local = expansion.astype(jnp.bfloat16)
    far_field = jnp.einsum('lkr,lrp->lkp', leaf_local.astype(jnp.float32), basis.astype(jnp.float32))
    return near + far_field
```

```python
import jax
import jax.numpy as jnp
from jax import lax
from jax.experimental import pallas as pl
from jax.experimental.pallas import tpu as pltpu
from jax.sharding import PartitionSpec as P

AREA_WEIGHT = 0.0625
SOFTENING = 0.0025
SCALE = 1.0 / AREA_WEIGHT

NK = 16
RANK = 32
LANES = 128
LEVELS = 7
F32 = jnp.float32
BF16 = jnp.bfloat16

NODES = [LANES >> level for level in range(8)]
FOLD = [min(NK, 1 << level) for level in range(8)]
PLANES = [NK // fold for fold in FOLD]
ROWS = [planes * RANK for planes in PLANES]
START = [sum(ROWS[:level]) for level in range(9)]
TILE_ROW = [0, 0, 64, 96, 112, 120, 124, 126]
HALO_LANE = [0, 2, 6, 14, 30, 62, 94]
M_ROWS = START[LEVELS]
HEAD = 24
FRAME = 8 * (LANES + 2)


def log2(value):
    return value.bit_length() - 1


def iota(shape, dim):
    return lax.broadcasted_iota(jnp.int32, shape, dim)


def ones_where(cond):
    return jnp.where(cond, 1.0, 0.0).astype(BF16)


def dot(a, b):
    return jnp.dot(a, b, preferred_element_type=F32)


def dot_nt(a, b):
    return lax.dot_general(a, b, (((1,), (1,)), ((), ())), preferred_element_type=F32)


def dot_tn(a, b):
    return lax.dot_general(a, b, (((0,), (0,)), ((), ())), preferred_element_type=F32)


def split(x):
    high = x.astype(BF16)
    low = (x - high.astype(F32)).astype(BF16)
    return high, low


def dot_exact(x, selection):
    high, low = split(x)
    return dot(high, selection) + dot(low, selection)


def eye():
    return ones_where(iota((LANES, LANES), 0) == iota((LANES, LANES), 1))


def pair_target(level, index):
    nodes = NODES[level]
    lane = index & (LANES - 1)
    node = lane & (nodes - 1)
    high = lane >> log2(nodes)
    if level < 4:
        half = index >> 7
        return high * nodes + half * (nodes // 2) + (node >> 1)
    return jnp.where(lane < NK * nodes, high * (nodes // 2) + (node >> 1), -1)


def pair_matrix(level):
    depth = 2 * LANES if level < 4 else LANES
    return ones_where(pair_target(level, iota((depth, LANES), 0)) == iota((depth, LANES), 1))


def pair_matrix_t(level):
    width = 2 * LANES if level < 4 else LANES
    return ones_where(pair_target(level, iota((LANES, width), 1)) == iota((LANES, width), 0))


def spread_matrix(level):
    nodes = NODES[level]
    row, lane = iota((LANES, LANES), 0), iota((LANES, LANES), 1)
    return ones_where((row == TILE_ROW[level] + (lane & (nodes - 1))) & (lane < FOLD[level] * nodes))


def turn_order():
    row, lane = iota((2 * LANES, 2 * LANES), 0), iota((2 * LANES, 2 * LANES), 1)
    return ones_where(row == (lane & (RANK - 1)) * 8 + (lane >> 5))


def transpose_swapped(order, rows_of, out_ref):
    for pair in range(4):
        turned = dot_nt(order, jnp.concatenate([rows_of(2 * pair), rows_of(2 * pair + 1)], axis=1))
        for t in range(RANK):
            out_ref[t * RANK + 8 * pair : t * RANK + 8 * pair + 8, :] = turned[8 * t : 8 * t + 8, :]


def extra_rows(four_ref, two_ref, d):
    four = pltpu.roll(four_ref[...].astype(F32), (8 - 4 * (d & 1)) & 7, 0)
    two = pltpu.roll(two_ref[...].astype(F32), (12 - 2 * (d & 3)) & 7, 0)
    row = iota((8, 1024), 0)
    return jnp.where(row < 4, four, jnp.where(row < 6, two, 0.0))


def head_rows(ref):
    return lambda c: ref[0:LANES, c * LANES : (c + 1) * LANES]


def tail_rows(ref, extra):
    def rows_of(c):
        cut = slice(c * LANES, (c + 1) * LANES)
        return jnp.concatenate([ref[LANES:248, cut].astype(F32), extra[:, cut]], axis=0).astype(BF16)

    return rows_of


def transpose_matrices(identity, rows_of, out_ref, base=0):
    for chunk in range(8):
        turned = dot_nt(identity, rows_of(chunk))
        out_ref[base + chunk * LANES : base + (chunk + 1) * LANES, :] = turned.astype(out_ref.dtype)


def spread_matrices(level, turned_ref, out_ref, base=0):
    spread = spread_matrix(level)
    for chunk in range(8):
        rows = slice(base + chunk * LANES, base + (chunk + 1) * LANES)
        out_ref[rows, :] = dot(turned_ref[rows, :].astype(BF16), spread)


def contract(plane_count, row_of, tile_of, store, init=None):
    block = min(4, plane_count)

    def run(first):
        if init is None:
            totals = [jnp.zeros((RANK, LANES), F32) for _ in range(block)]
        else:
            totals = [init(first + p) for p in range(block)]
        for r in range(RANK):
            tile = tile_of(r)
            for p in range(block):
                totals[p] = totals[p] + row_of(first + p, r) * tile
        for p in range(block):
            store(first + p, totals[p])

    if plane_count == block:
        run(0)
    else:
        lax.fori_loop(0, plane_count // block, lambda b, c: (run(b * block), c)[1], 0)


def plane_rows(plane):
    if isinstance(plane, int):
        return slice(plane * RANK, (plane + 1) * RANK)
    return pl.ds(pl.multiple_of(plane * RANK, RANK), RANK)


def climb(level, m_ref, source_base, matrix_ref, x_ref):
    def row_of(plane, r):
        return m_ref[pl.ds(source_base + plane * RANK + r, 1), :]

    def tile_of(r):
        return matrix_ref[r * RANK : (r + 1) * RANK, :]

    def store(plane, value):
        x_ref[plane_rows(plane), :] = value

    contract(PLANES[level], row_of, tile_of, store)


def pair_sum(level, x_ref):
    if level < 4:
        half = ROWS[level] // 2
        x = jnp.concatenate([x_ref[0:half, :], x_ref[half : 2 * half, :]], axis=1)
    else:
        x = x_ref[0:RANK, :]
    return dot_exact(x, pair_matrix(level))


def up_kernel(
    par_ref, ch_ref, pt_ref, ba_ref, e_ref, four_ref, two_ref, m_ref, near_msg, far_msg, top_ref, y_ref, x_ref, t_ref, w_ref
):
    d = par_ref[0]
    odd = d & 1
    first_leaf = [pt_ref[:, 0, :], ch_ref[0].astype(F32)]
    last_leaf = [pt_ref[:, LANES - 1, :], ch_ref[LANES - 1].astype(F32)]
    near_msg[0:HEAD, :] = jnp.zeros((HEAD, LANES), F32)
    far_msg[0:HEAD, :] = jnp.zeros((HEAD, LANES), F32)
    for rows, first, last in zip((slice(0, 3), slice(8, 24)), first_leaf, last_leaf):
        near_msg[rows, :] = jnp.where(odd == 1, first, last)
        far_msg[rows, :] = jnp.where(odd == 1, last, first)

    def leaf(i, carry):
        y_ref[pl.ds(pl.multiple_of(i * NK, NK), NK), 0:RANK] = dot_nt(ch_ref[i], ba_ref[i])
        return carry

    lax.fori_loop(0, LANES, leaf, 0, unroll=8)
    identity = eye()
    transpose_matrices(identity, head_rows(e_ref), w_ref)
    transpose_matrices(identity, tail_rows(e_ref, extra_rows(four_ref, two_ref, d)), t_ref)
    for k in range(NK):
        m_ref[k * RANK : (k + 1) * RANK, :] = y_ref[pl.ds(k, LANES, stride=NK), :].T[0:RANK, :]
    for level in range(LEVELS):
        if level > 0:
            spread_matrices(level, t_ref, w_ref)
        climb(level, m_ref, START[level], w_ref, x_ref)
        if level < LEVELS - 1:
            m_ref[START[level + 1] : START[level + 2], :] = pair_sum(level, x_ref)
    row, lane = iota((LANES, LANES), 0), iota((LANES, LANES), 1)
    spread = ones_where(((row >> 1) == (lane & (NK - 1))) & (row < 2 * NK))
    device = dot_exact(x_ref[0:RANK, :], spread)
    sub, lane8 = iota((8, LANES), 0), iota((8, LANES), 1)
    for a in range(4):
        kept = jnp.where(sub == (lane8 >> 4), device[8 * a : 8 * a + 8, :], 0.0)
        top_ref[:, a * LANES : (a + 1) * LANES] = jnp.broadcast_to(jnp.sum(kept, axis=0, keepdims=True), (LANES, LANES))
    for level in reversed(range(LEVELS)):
        nodes = NODES[level]
        row, lane = iota((LANES, 2 * LANES), 0), iota((LANES, 2 * LANES), 1)
        first = odd ^ (lane >> 7)
        slot = (lane & (LANES - 1)) - HALO_LANE[level]
        node = (slot & 1) + jnp.where(first == 1, 0, nodes - 2)
        wanted = (slot >> 1) * nodes + node
        pick = ones_where((slot >= 0) & (slot < 2 * FOLD[level]) & (row == wanted))
        picked = dot_exact(m_ref[START[level] : START[level + 1], :], pick)
        if level == LEVELS - 1:
            near_msg[HEAD:, :] = jnp.zeros((ROWS[0], LANES), F32)
            far_msg[HEAD:, :] = jnp.zeros((ROWS[0], LANES), F32)
        near_msg[HEAD : HEAD + ROWS[level], :] += picked[:, 0:LANES]
        far_msg[HEAD : HEAD + ROWS[level], :] += picked[:, LANES : 2 * LANES]


def couple_kernel(
    par_ref, m_ref, near_ref, far_ref, list_ref, top_list, s_ref, four_ref, two_ref, out_ref, src_ref, t_ref, w_ref, rel_ref
):
    d = par_ref[0]
    odd = (d & 1) == 1
    place = iota((1, LANES), 1)
    rel_ref[...] = jnp.full((8, 2 * LANES), 64.0, F32)
    start = jnp.where(place < 64, 0, jnp.where(place < 96, 64, jnp.where(place < 112, 96, 112)))
    count = jnp.where(place < 64, 64, jnp.where(place < 96, 32, jnp.where(place < 112, 16, 8)))
    for s in range(3):
        fine = list_ref[s, :, 0:LANES]
        rel_ref[s : s + 1, 0:LANES] = jnp.where(fine >= 0, fine - (d * LANES + place), 64).astype(F32)
        rest = list_ref[s, :, LANES:248]
        own = (d * count + place - start)[:, 0:120]
        rel_ref[s : s + 1, LANES:248] = jnp.where(rest >= 0, rest - own, 64).astype(F32)
        row = rel_ref[s : s + 1, LANES : 2 * LANES]
        for lane_at, base, nodes in ((120, 4 * d, 4), (124, 512 + 2 * d, 2)):
            for t in range(nodes):
                entry = top_list[s, base + t]
                index = (4 * d if nodes == 4 else 2 * d) + t
                value = jnp.where(entry >= 0, entry - index, 64).astype(F32)
                row = jnp.where(place == lane_at + t, value, row)
        rel_ref[s : s + 1, LANES : 2 * LANES] = row
    identity = eye()
    row = iota((LANES, LANES), 0)
    lane = iota((1, LANES), 1)
    for level in range(LEVELS):
        nodes, rows = NODES[level], ROWS[level]
        tile = 0 if level == 0 else 1
        for s in range(3):
            if level == 0:
                transpose_matrices(identity, head_rows(s_ref.at[s]), w_ref, s * 1024)
                extra = extra_rows(four_ref.at[s], two_ref.at[s], d)
                transpose_matrices(identity, tail_rows(s_ref.at[s], extra), t_ref, s * 1024)
            else:
                spread_matrices(level, t_ref, w_ref, s * 1024)
        rel = rel_ref[:, tile * LANES : (tile + 1) * LANES]
        if level > 0:
            rel = dot(rel.astype(BF16), spread_matrix(level))
        rel = rel.astype(jnp.int32)
        moments = m_ref[START[level] : START[level + 1], :]
        near_part, far_part = near_ref[HEAD : HEAD + rows, :], far_ref[HEAD : HEAD + rows, :]
        left = split(jnp.where(odd, near_part, far_part))
        right = split(jnp.where(odd, far_part, near_part))
        own = split(moments)
        node = lane & (nodes - 1)
        high = lane >> log2(nodes)
        for s in range(3):
            shift = rel[s : s + 1, :]
            target = node + shift
            usable = (shift >= -3) & (shift <= 3)
            inside = usable & (target >= 0) & (target < nodes)
            at_own = jnp.where(inside, high * nodes + target, -1)
            at_left = jnp.where(usable & (target < 0), HALO_LANE[level] + 2 * high + target + 2, -1)
            at_right = jnp.where(usable & (target >= nodes), HALO_LANE[level] + 2 * high + target - nodes, -1)
            total = None
            for part, at in ((own, at_own), (left, at_left), (right, at_right)):
                pick = ones_where(row == at)
                piece = dot(part[0], pick) + dot(part[1], pick)
                total = piece if total is None else total + piece
            src_ref[s * 512 : s * 512 + rows, :] = total

        base = START[level]

        def init(plane):
            return jnp.zeros((RANK, LANES), F32)

        def store(plane, value):
            out_ref[pl.ds(pl.multiple_of(base + plane * RANK, RANK), RANK), :] = value

        block = min(4, PLANES[level])

        def run(first):
            def slot(s, totals):
                totals = list(totals)
                for r in range(RANK):
                    tile_rows = w_ref[pl.ds(pl.multiple_of(s * 1024 + r * RANK, RANK), RANK), :]
                    for p in range(block):
                        at = s * 512 + (first + p) * RANK + r
                        totals[p] = totals[p] + src_ref[pl.ds(at, 1), :] * tile_rows
                return tuple(totals)

            totals = lax.fori_loop(0, 3, slot, tuple(init(p) for p in range(block)))
            for p in range(block):
                store(first + p, totals[p])

        if PLANES[level] == block:
            run(0)
        else:
            lax.fori_loop(0, PLANES[level] // block, lambda b, c: (run(b * block), c)[1], 0)


def top_kernel(par_ref, list_ref, g_ref, e_ref, s_ref, out_ref, m0_ref, m_ref, x_ref, t_ref, w_ref, src_ref, so_t, eo_t):
    d = par_ref[0]
    identity = eye()
    for a in range(4):
        m0_ref[a * LANES : (a + 1) * LANES, :] = g_ref[:, a * LANES : (a + 1) * LANES].T
    for k in range(NK):
        m_ref[k * RANK : (k + 1) * RANK, :] = m0_ref[pl.ds(k, RANK, stride=NK), :]
    transpose_matrices(identity, lambda c: e_ref[0:LANES, c * LANES : (c + 1) * LANES], w_ref)
    known = iota((LANES, LANES), 0) < 120

    def last_rows(c):
        block = e_ref[LANES : 2 * LANES, c * LANES : (c + 1) * LANES].astype(F32)
        return jnp.where(known, block, 0.0).astype(BF16)

    transpose_matrices(identity, last_rows, t_ref)
    row, lane = iota((LANES, 2 * LANES), 0), iota((LANES, 2 * LANES), 1)
    level_of = row >> 4
    own_lane = jnp.where(level_of == 5, 248 + (d >> 5), -1)
    for level in range(5):
        own_lane = jnp.where(level_of == level, 256 - (256 >> level) + (d >> level), own_lane)
    own_rows = ones_where(lane == own_lane)
    filled = iota((2 * LANES, LANES), 0)

    def own_of(ref, rows):
        def rows_of(c):
            block = ref[:, c * LANES : (c + 1) * LANES].astype(F32)
            return dot(own_rows, jnp.where(filled < rows, block, 0.0).astype(BF16)).astype(BF16)

        return rows_of

    for s in range(3):
        transpose_matrices(identity, own_of(s_ref.at[s], 252), so_t, s * 1024)
    transpose_swapped(turn_order(), own_of(e_ref, 248), eo_t)
    for level in range(5):
        if level > 0:
            spread_matrices(level, t_ref, w_ref)
        climb(level, m_ref, START[level], w_ref, x_ref)
        m_ref[START[level + 1] : START[level + 2], :] = pair_sum(level, x_ref)
    row, lane = iota((LANES, LANES), 0), iota((LANES, LANES), 1)
    lane_r = iota((RANK, LANES), 1)
    sources = [jnp.zeros((RANK, LANES), F32) for _ in range(3)]
    for level in range(6):
        planes = PLANES[level]
        high = (lane & (NK - 1)) >> log2(planes)
        delta = row - high * NODES[level]
        here = (lane >> 4) == level
        entries = [list_ref[s, 1024 - (256 >> level) + (d >> level)] for s in range(3)]
        picks = [ones_where(here & (delta == jnp.where(e >= 0, e, -100000))) for e in entries]
        found = dot_exact(m_ref[START[level] : START[level + 1], :], jnp.concatenate(picks, axis=1))
        for plane in range(planes):
            mine = (lane_r & (planes - 1)) == plane
            for s in range(3):
                part = found[plane * RANK : (plane + 1) * RANK, s * LANES : (s + 1) * LANES]
                sources[s] = sources[s] + jnp.where(mine, part, 0.0)
    coupled = jnp.zeros((RANK, LANES), F32)
    for s in range(3):
        src_ref[s * RANK : (s + 1) * RANK, :] = sources[s]
    for s in range(3):
        for r in range(RANK):
            at = s * 1024 + r * RANK
            coupled = coupled + src_ref[s * RANK + r : s * RANK + r + 1, :] * so_t[at : at + RANK, :]
    local = coupled
    for level in reversed(range(5)):
        src_ref[0:RANK, :] = pltpu.roll(local, LANES - NK, 1)
        local = coupled
        for t in range(RANK):
            local = local + src_ref[t : t + 1, :] * eo_t[t * RANK : (t + 1) * RANK, :]
    out_ref[...] = local


def down_kernel(
    par_ref, top_ref, c_ref, e_ref, four_ref, two_ref, ba_ref, near_ref, out_ref, l_ref, p_ref, z_ref, t_ref, w_ref
):
    order = turn_order()
    transpose_swapped(order, tail_rows(e_ref, extra_rows(four_ref, two_ref, par_ref[0])), t_ref)
    l_ref[0:RANK, :] = top_ref[...]
    for level in reversed(range(LEVELS)):
        if level > 0:
            spread_matrices(level, t_ref, w_ref)
        else:
            transpose_swapped(order, head_rows(e_ref), w_ref)
        given = dot_exact(l_ref[0 : ROWS[level + 1], :], pair_matrix_t(level))
        if level < 4:
            half = ROWS[level + 1]
            p_ref[0:half, :] = given[:, 0:LANES]
            p_ref[half : 2 * half, :] = given[:, LANES : 2 * LANES]
        else:
            p_ref[0:RANK, :] = given

        def row_of(plane, t):
            return p_ref[pl.ds(plane * RANK + t, 1), :]

        def tile_of(t):
            return w_ref[t * RANK : (t + 1) * RANK, :]

        def init(plane):
            return c_ref[pl.ds(START[level] + plane * RANK, RANK), :]

        def store(plane, value):
            l_ref[plane_rows(plane), :] = value

        contract(PLANES[level], row_of, tile_of, store, init)
    for k in range(NK):
        z_ref[pl.ds(k, LANES, stride=NK), 0:RANK] = l_ref[k * RANK : (k + 1) * RANK, :].T

    def leaf(i, carry):
        local = z_ref[pl.ds(pl.multiple_of(i * NK, NK), NK), 0:RANK].astype(BF16)
        out_ref[i] = near_ref[i] + dot(local, ba_ref[i])
        return carry

    lax.fori_loop(0, LANES, leaf, 0, unroll=8)


def three(x):
    first = x.astype(BF16).astype(F32)
    rest = x - first
    second = rest.astype(BF16).astype(F32)
    return first, second, (rest - second).astype(BF16).astype(F32)


def near_kernel(par_ref, list_ref, pt_ref, ch_ref, near_msg, far_msg, out_ref, fa_ref, fs_ref, fn_ref, k_ref):
    d = par_ref[0]
    odd = (d & 1) == 1
    base = d * LANES
    left = jnp.where(odd, near_msg[...], far_msg[...])
    right = jnp.where(odd, far_msg[...], near_msg[...])
    soft = jnp.float32(SOFTENING) * (SCALE * SCALE)
    row8 = iota((FRAME, LANES), 0) & 7
    fa_ref[...] = jnp.where(row8 == 4, 1.0, 0.0)
    fs_ref[...] = jnp.where(row8 == 3, 1.0, 0.0)
    fn_ref[...] = jnp.where(row8 == 3, 1.0, 0.0)

    def features(values, first_leaf, put):
        x = ((values[0] - first_leaf.astype(F32)) - 0.5) * SCALE
        y, z = (values[1] - 0.5) * SCALE, (values[2] - 0.5) * SCALE
        moved = x + SCALE
        flat = y * y + z * z
        for j, value in enumerate((x, y, z, x * x + flat)):
            put(fa_ref, j, value)
        for ref, along in ((fs_ref, x), (fn_ref, moved)):
            for j, value in ((0, -2.0 * along), (1, -2.0 * y), (2, -2.0 * z), (4, along * along + flat + soft)):
                put(ref, j, value)

    def put_own(ref, j, value):
        ref[pl.ds(8 + j, LANES, stride=8), :] = value

    def put_left(ref, j, value):
        ref[j : j + 1, :] = value

    def put_right(ref, j, value):
        at = (LANES + 1) * 8 + j
        ref[at : at + 1, :] = value

    features([pt_ref[0], pt_ref[1], pt_ref[2]], iota((LANES, LANES), 0) + base, put_own)
    one_leaf = iota((1, LANES), 0) + base
    features([left[c : c + 1, :] for c in range(3)], one_leaf - 1, put_left)
    features([right[c : c + 1, :] for c in range(3)], one_leaf + LANES, put_right)

    def lists(i, offset):
        wanted = base + i + offset
        hit = (list_ref[0, i] == wanted) | (list_ref[1, i] == wanted) | (list_ref[2, i] == wanted)
        return jnp.where(hit, 1.0, 0.0).astype(F32)

    def pieces(ref, w):
        return three(ref[pl.ds(pl.multiple_of(w * 8, 8), 8), :])

    def source_of(w):
        a, b, c = pieces(fa_ref, w)
        return jnp.concatenate([a, a, b, b, a, c], axis=0).astype(BF16)

    def target_of(ref, w):
        a, b, c = pieces(ref, w)
        return jnp.concatenate([a, b, a, b, c, a], axis=0).astype(BF16)

    def kernel_of(source, target):
        return lax.rsqrt(dot_tn(source, target)).astype(BF16)

    first = dot(left[8:24, :].astype(BF16), kernel_of(source_of(0), target_of(fn_ref, 1)))

    def fill(i, carry):
        both = jnp.concatenate([target_of(fs_ref, i + 1), target_of(fn_ref, i + 2)], axis=1)
        k_ref[i] = kernel_of(source_of(i + 1), both)
        return carry

    lax.fori_loop(0, LANES, fill, 0, unroll=16)

    def step(i, carry, own, after):
        spread = dot(own, k_ref[i])
        back = dot_nt(after, k_ref[i, :, LANES : 2 * LANES])
        out_ref[i] = carry + spread[:, 0:LANES] + lists(i, 1) * back
        return spread[:, LANES : 2 * LANES]

    def body(i, carry):
        onward = step(i, carry, ch_ref[i], ch_ref[i + 1])
        return lists(i + 1, -1) * onward

    carry = lax.fori_loop(0, LANES - 1, body, lists(0, -1) * first, unroll=16)
    step(LANES - 1, carry, ch_ref[LANES - 1], right[8:24, :].astype(BF16))


VMEM = pl.BlockSpec(memory_space=pltpu.VMEM)
SMEM = pl.BlockSpec(memory_space=pltpu.SMEM)


def scratch(*shape, dtype=F32):
    return pltpu.VMEM(shape, dtype)


def shape(*dims):
    return jax.ShapeDtypeStruct(dims, F32)


def whole(*dims):
    return pl.BlockSpec(dims, lambda i, par: (0,) * len(dims))


NEAR_SCRATCH = [scratch(FRAME, LANES)] * 3 + [scratch(LANES, LANES, 2 * LANES, dtype=BF16)]
FOUR = pl.BlockSpec((8, 1024), lambda i, par: (par[0] >> 1, 0))
TWO = pl.BlockSpec((8, 1024), lambda i, par: (64 + (par[0] >> 2), 0))
FOUR_C = pl.BlockSpec((3, 8, 1024), lambda i, par: (0, par[0] >> 1, 0))
TWO_C = pl.BlockSpec((3, 8, 1024), lambda i, par: (0, 64 + (par[0] >> 2), 0))
LEAF_SPEC = pl.BlockSpec((HEAD, LANES), lambda i, par: (0, 0))


def call(kernel, name, in_specs, out_specs, out_shape, scratch_shapes):
    return pl.pallas_call(
        kernel,
        name=name,
        grid_spec=pltpu.PrefetchScalarGridSpec(
            num_scalar_prefetch=1,
            grid=(1,),
            in_specs=in_specs,
            out_specs=out_specs,
            scratch_shapes=scratch_shapes,
        ),
        out_shape=out_shape,
    )


def on_device(
    charges, points, basis, near_list, loc_coupling, loc_transfer, loc_lists, top_coupling, top_transfer, top_lists
):
    devices = lax.axis_size("cluster")
    d = lax.axis_index("cluster")
    mates = [(i, i ^ 1) for i in range(devices)]
    others = [(i, ((i + 1) ^ 1) - 1) for i in range(devices) if 0 <= ((i + 1) ^ 1) - 1 < devices]
    par = d.astype(jnp.int32).reshape(1)
    points_t = jnp.transpose(points, (1, 0, 2))
    transfer = loc_transfer[0]
    coupling = jnp.transpose(loc_coupling[0], (1, 0, 2))
    top_c = jnp.transpose(top_coupling, (1, 0, 2))
    top_l = jnp.transpose(top_lists)
    message = HEAD + ROWS[0]
    moments, msg_near, msg_far, device_moment = call(
        up_kernel,
        "up",
        [whole(LANES, NK, LANES), whole(3, LANES, LANES), whole(LANES, RANK, LANES), whole(248, 1024), FOUR, TWO],
        [whole(M_ROWS, LANES), whole(message, LANES), whole(message, LANES), whole(LANES, 512)],
        [shape(M_ROWS, LANES), shape(message, LANES), shape(message, LANES), shape(LANES, 512)],
        [scratch(2048, LANES), scratch(512, LANES), scratch(1024, LANES, dtype=BF16), scratch(1024, LANES)],
    )(par, charges, points_t, basis, transfer, top_transfer, top_transfer)

    halo_near = lax.ppermute(msg_near, "cluster", mates)
    halo_far = lax.ppermute(msg_far, "cluster", others)
    gathered = lax.all_to_all(device_moment, "cluster", 0, 0, tiled=True)

    near = call(
        near_kernel,
        "near",
        [SMEM, whole(3, LANES, LANES), whole(LANES, NK, LANES), LEAF_SPEC, LEAF_SPEC],
        whole(LANES, NK, LANES),
        shape(LANES, NK, LANES),
        NEAR_SCRATCH,
    )(par, near_list.T, points_t, charges, halo_near, halo_far)

    coupled = call(
        couple_kernel,
        "couple",
        [
            whole(M_ROWS, LANES),
            whole(message, LANES),
            whole(message, LANES),
            whole(3, 1, 248),
            SMEM,
            whole(3, 248, 1024),
            FOUR_C,
            TWO_C,
        ],
        whole(M_ROWS, LANES),
        shape(M_ROWS, LANES),
        [scratch(1536, LANES), scratch(3072, LANES, dtype=BF16), scratch(3072, LANES), scratch(8, 2 * LANES)],
    )(par, moments, halo_near, halo_far, jnp.transpose(loc_lists, (2, 0, 1)), top_l, coupling, top_c, top_c)

    top_local = call(
        top_kernel,
        "top",
        [
            SMEM,
            whole(LANES, 512),
            pl.BlockSpec((256, 1024), lambda i, par: (3, 0)),
            pl.BlockSpec((3, 256, 1024), lambda i, par: (0, 3, 0)),
        ],
        whole(RANK, LANES),
        shape(RANK, LANES),
        [
            scratch(512, LANES),
            scratch(START[6], LANES),
            scratch(512, LANES),
            scratch(1024, LANES, dtype=BF16),
            scratch(1024, LANES),
            scratch(96, LANES),
            scratch(3072, LANES),
            scratch(1024, LANES),
        ],
    )(par, top_l, gathered, top_transfer, top_c)

    return call(
        down_kernel,
        "down",
        [
            whole(RANK, LANES),
            whole(M_ROWS, LANES),
            whole(248, 1024),
            FOUR,
            TWO,
            whole(LANES, RANK, LANES),
            whole(LANES, NK, LANES),
        ],
        whole(LANES, NK, LANES),
        shape(LANES, NK, LANES),
        [
            scratch(512, LANES),
            scratch(512, LANES),
            scratch(2048, LANES),
            scratch(1024, LANES),
            scratch(1024, LANES),
        ],
    )(par, top_local, coupled, transfer, top_transfer, top_transfer, basis, near)


def solution(mesh):
    placed = (
        P("cluster", None, None),
        P("cluster", None, None),
        P("cluster", None, None),
        P("cluster", None),
        P("cluster", None, None, None),
        P("cluster", None, None),
        P("cluster", None, None),
        P(),
        P(),
        P(),
    )
    return jax.shard_map(
        on_device, mesh=mesh, in_specs=placed, out_specs=P("cluster", None, None), check_vma=False
    )
```

```python
import functools

import jax
import jax.numpy as jnp
from jax import lax
from jax.experimental import pallas as pl
from jax.experimental.pallas import tpu as pltpu
from jax.sharding import PartitionSpec as P


AREA_WEIGHT = 0.0625
SOFTENING = 0.0025
SCALE = 1.0 / AREA_WEIGHT

NK = 16
RANK = 32
LANES = 128
LEVELS = 7
F32 = jnp.float32
BF16 = jnp.bfloat16

NODES = [LANES >> level for level in range(8)]
FOLD = [min(NK, 1 << level) for level in range(8)]
PLANES = [NK // fold for fold in FOLD]
ROWS = [planes * RANK for planes in PLANES]
START = [sum(ROWS[:level]) for level in range(9)]
TILE_ROW = [0, 0, 64, 96, 112, 120, 124, 126]
HALO_LANE = [0, 2, 6, 14, 30, 62, 94]
M_ROWS = START[LEVELS]
HEAD = 24
PART = 32
PARTS = LANES // PART
AHEAD = 8
FRAME = 8 * (PART + 2)


def log2(value):
    return value.bit_length() - 1


def iota(shape, dim):
    return lax.broadcasted_iota(jnp.int32, shape, dim)


def ones_where(cond):
    return jnp.where(cond, 1.0, 0.0).astype(BF16)


def dot(a, b):
    return jnp.dot(a, b, preferred_element_type=F32)


def dot_nt(a, b):
    return lax.dot_general(a, b, (((1,), (1,)), ((), ())), preferred_element_type=F32)


def dot_tn(a, b):
    return lax.dot_general(a, b, (((0,), (0,)), ((), ())), preferred_element_type=F32)


def split(x):
    high = x.astype(BF16)
    low = (x - high.astype(F32)).astype(BF16)
    return high, low


def dot_exact(x, selection):
    high, low = split(x)
    return dot(high, selection) + dot(low, selection)


def eye():
    return ones_where(iota((LANES, LANES), 0) == iota((LANES, LANES), 1))


def pair_target(level, index):
    nodes = NODES[level]
    lane = index & (LANES - 1)
    node = lane & (nodes - 1)
    high = lane >> log2(nodes)
    if level < 4:
        half = index >> 7
        return high * nodes + half * (nodes // 2) + (node >> 1)
    return jnp.where(lane < NK * nodes, high * (nodes // 2) + (node >> 1), -1)


def pair_matrix(level):
    depth = 2 * LANES if level < 4 else LANES
    return ones_where(pair_target(level, iota((depth, LANES), 0)) == iota((depth, LANES), 1))


def pair_matrix_t(level):
    width = 2 * LANES if level < 4 else LANES
    return ones_where(pair_target(level, iota((LANES, width), 1)) == iota((LANES, width), 0))


def spread_matrix(level):
    nodes = NODES[level]
    row, lane = iota((LANES, LANES), 0), iota((LANES, LANES), 1)
    return ones_where((row == TILE_ROW[level] + (lane & (nodes - 1))) & (lane < FOLD[level] * nodes))


def turn_order():
    row, lane = iota((2 * LANES, 2 * LANES), 0), iota((2 * LANES, 2 * LANES), 1)
    return ones_where(row == (lane & (RANK - 1)) * 8 + (lane >> 5))


def transpose_swapped(order, rows_of, out_ref):
    for pair in range(4):
        turned = dot_nt(order, jnp.concatenate([rows_of(2 * pair), rows_of(2 * pair + 1)], axis=1))
        for t in range(RANK):
            out_ref[t * RANK + 8 * pair : t * RANK + 8 * pair + 8, :] = turned[8 * t : 8 * t + 8, :]


def extra_rows(four_ref, two_ref, d):
    four = pltpu.roll(four_ref[...].astype(F32), (8 - 4 * (d & 1)) & 7, 0)
    two = pltpu.roll(two_ref[...].astype(F32), (12 - 2 * (d & 3)) & 7, 0)
    row = iota((8, 1024), 0)
    return jnp.where(row < 4, four, jnp.where(row < 6, two, 0.0))


def head_rows(ref):
    return lambda c: ref[0:LANES, c * LANES : (c + 1) * LANES]


def tail_rows(ref, extra):
    def rows_of(c):
        cut = slice(c * LANES, (c + 1) * LANES)
        return jnp.concatenate([ref[LANES:248, cut].astype(F32), extra[:, cut]], axis=0).astype(BF16)

    return rows_of


def transpose_matrices(identity, rows_of, out_ref, base=0):
    for chunk in range(8):
        turned = dot_nt(identity, rows_of(chunk))
        out_ref[base + chunk * LANES : base + (chunk + 1) * LANES, :] = turned.astype(out_ref.dtype)


def spread_matrices(level, turned_ref, out_ref, base=0):
    spread = spread_matrix(level)
    for chunk in range(8):
        rows = slice(base + chunk * LANES, base + (chunk + 1) * LANES)
        out_ref[rows, :] = dot(turned_ref[rows, :].astype(BF16), spread)


def contract(plane_count, row_of, tile_of, store, init=None):
    block = min(4, plane_count)

    def run(first):
        if init is None:
            totals = [jnp.zeros((RANK, LANES), F32) for _ in range(block)]
        else:
            totals = [init(first + p) for p in range(block)]
        for r in range(RANK):
            tile = tile_of(r)
            for p in range(block):
                totals[p] = totals[p] + row_of(first + p, r) * tile
        for p in range(block):
            store(first + p, totals[p])

    if plane_count == block:
        run(0)
    else:
        lax.fori_loop(0, plane_count // block, lambda b, c: (run(b * block), c)[1], 0)


def plane_rows(plane):
    if isinstance(plane, int):
        return slice(plane * RANK, (plane + 1) * RANK)
    return pl.ds(pl.multiple_of(plane * RANK, RANK), RANK)


def climb(level, m_ref, source_base, matrix_ref, x_ref):
    def row_of(plane, r):
        return m_ref[pl.ds(source_base + plane * RANK + r, 1), :]

    def tile_of(r):
        return matrix_ref[r * RANK : (r + 1) * RANK, :]

    def store(plane, value):
        x_ref[plane_rows(plane), :] = value

    contract(PLANES[level], row_of, tile_of, store)


def pair_sum(level, x_ref):
    if level < 4:
        half = ROWS[level] // 2
        x = jnp.concatenate([x_ref[0:half, :], x_ref[half : 2 * half, :]], axis=1)
    else:
        x = x_ref[0:RANK, :]
    return dot_exact(x, pair_matrix(level))


def up_kernel(
    par_ref, ch_ref, pt_ref, ba_ref, e_ref, four_ref, two_ref, m_ref, near_msg, far_msg, top_ref, y_ref, x_ref, t_ref, w_ref
):
    d = par_ref[0]
    odd = d & 1
    first_leaf = [pt_ref[:, 0, :], ch_ref[0].astype(F32)]
    last_leaf = [pt_ref[:, LANES - 1, :], ch_ref[LANES - 1].astype(F32)]
    near_msg[0:HEAD, :] = jnp.zeros((HEAD, LANES), F32)
    far_msg[0:HEAD, :] = jnp.zeros((HEAD, LANES), F32)
    for rows, first, last in zip((slice(0, 3), slice(8, 24)), first_leaf, last_leaf):
        near_msg[rows, :] = jnp.where(odd == 1, first, last)
        far_msg[rows, :] = jnp.where(odd == 1, last, first)

    def leaf(i, carry):
        y_ref[pl.ds(pl.multiple_of(i * NK, NK), NK), 0:RANK] = dot_nt(ch_ref[i], ba_ref[i])
        return carry

    lax.fori_loop(0, LANES, leaf, 0, unroll=8)
    identity = eye()
    transpose_matrices(identity, head_rows(e_ref), w_ref)
    transpose_matrices(identity, tail_rows(e_ref, extra_rows(four_ref, two_ref, d)), t_ref)
    for k in range(NK):
        m_ref[k * RANK : (k + 1) * RANK, :] = y_ref[pl.ds(k, LANES, stride=NK), :].T[0:RANK, :]
    for level in range(LEVELS):
        if level > 0:
            spread_matrices(level, t_ref, w_ref)
        climb(level, m_ref, START[level], w_ref, x_ref)
        if level < LEVELS - 1:
            m_ref[START[level + 1] : START[level + 2], :] = pair_sum(level, x_ref)
    row, lane = iota((LANES, LANES), 0), iota((LANES, LANES), 1)
    spread = ones_where(((row >> 1) == (lane & (NK - 1))) & (row < 2 * NK))
    device = dot_exact(x_ref[0:RANK, :], spread)
    sub, lane8 = iota((8, LANES), 0), iota((8, LANES), 1)
    for a in range(4):
        kept = jnp.where(sub == (lane8 >> 4), device[8 * a : 8 * a + 8, :], 0.0)
        top_ref[:, a * LANES : (a + 1) * LANES] = jnp.sum(kept, axis=0, keepdims=True)
    for level in reversed(range(LEVELS)):
        nodes = NODES[level]
        row, lane = iota((LANES, 2 * LANES), 0), iota((LANES, 2 * LANES), 1)
        first = odd ^ (lane >> 7)
        slot = (lane & (LANES - 1)) - HALO_LANE[level]
        node = (slot & 1) + jnp.where(first == 1, 0, nodes - 2)
        wanted = (slot >> 1) * nodes + node
        pick = ones_where((slot >= 0) & (slot < 2 * FOLD[level]) & (row == wanted))
        picked = dot_exact(m_ref[START[level] : START[level + 1], :], pick)
        if level == LEVELS - 1:
            near_msg[HEAD:, :] = jnp.zeros((ROWS[0], LANES), F32)
            far_msg[HEAD:, :] = jnp.zeros((ROWS[0], LANES), F32)
        near_msg[HEAD : HEAD + ROWS[level], :] += picked[:, 0:LANES]
        far_msg[HEAD : HEAD + ROWS[level], :] += picked[:, LANES : 2 * LANES]


def couple_kernel(
    levels,
    par_ref, m_ref, near_ref, far_ref, list_ref, top_list, s_ref, four_ref, two_ref, out_ref, src_ref, t_ref, w_ref, rel_ref
):
    d = par_ref[0]
    odd = (d & 1) == 1
    place = iota((1, LANES), 1)
    rel_ref[...] = jnp.full((8, 2 * LANES), 64.0, F32)
    start = jnp.where(place < 64, 0, jnp.where(place < 96, 64, jnp.where(place < 112, 96, 112)))
    count = jnp.where(place < 64, 64, jnp.where(place < 96, 32, jnp.where(place < 112, 16, 8)))
    for s in range(3):
        fine = list_ref[s, :, 0:LANES]
        rel_ref[s : s + 1, 0:LANES] = jnp.where(fine >= 0, fine - (d * LANES + place), 64).astype(F32)
        rest = list_ref[s, :, LANES:248]
        own = (d * count + place - start)[:, 0:120]
        rel_ref[s : s + 1, LANES:248] = jnp.where(rest >= 0, rest - own, 64).astype(F32)
        row = rel_ref[s : s + 1, LANES : 2 * LANES]
        for lane_at, base, nodes in ((120, 4 * d, 4), (124, 512 + 2 * d, 2)):
            for t in range(nodes):
                entry = top_list[s, base + t]
                index = (4 * d if nodes == 4 else 2 * d) + t
                value = jnp.where(entry >= 0, entry - index, 64).astype(F32)
                row = jnp.where(place == lane_at + t, value, row)
        rel_ref[s : s + 1, LANES : 2 * LANES] = row
    identity = eye()
    row = iota((LANES, LANES), 0)
    lane = iota((1, LANES), 1)
    shift_rows = START[levels[0]]
    if levels[0] > 0:
        for s in range(3):
            extra = extra_rows(four_ref.at[s], two_ref.at[s], d)
            transpose_matrices(identity, tail_rows(s_ref.at[s], extra), t_ref, s * 1024)
    for level in levels:
        nodes, rows = NODES[level], ROWS[level]
        tile = 0 if level == 0 else 1
        for s in range(3):
            if level == 0:
                transpose_matrices(identity, head_rows(s_ref.at[s]), w_ref, s * 1024)
            else:
                spread_matrices(level, t_ref, w_ref, s * 1024)
        rel = rel_ref[:, tile * LANES : (tile + 1) * LANES]
        if level > 0:
            rel = dot(rel.astype(BF16), spread_matrix(level))
        rel = rel.astype(jnp.int32)
        moments = m_ref[START[level] : START[level + 1], :]
        near_part, far_part = near_ref[HEAD : HEAD + rows, :], far_ref[HEAD : HEAD + rows, :]
        left = split(jnp.where(odd, near_part, far_part))
        right = split(jnp.where(odd, far_part, near_part))
        own = split(moments)
        node = lane & (nodes - 1)
        high = lane >> log2(nodes)
        for s in range(3):
            shift = rel[s : s + 1, :]
            target = node + shift
            usable = (shift >= -3) & (shift <= 3)
            inside = usable & (target >= 0) & (target < nodes)
            at_own = jnp.where(inside, high * nodes + target, -1)
            at_left = jnp.where(usable & (target < 0), HALO_LANE[level] + 2 * high + target + 2, -1)
            at_right = jnp.where(usable & (target >= nodes), HALO_LANE[level] + 2 * high + target - nodes, -1)
            total = None
            for part, at in ((own, at_own), (left, at_left), (right, at_right)):
                pick = ones_where(row == at)
                piece = dot(part[0], pick) + dot(part[1], pick)
                total = piece if total is None else total + piece
            src_ref[s * 512 : s * 512 + rows, :] = total

        base = START[level] - shift_rows

        def init():
            return jnp.zeros((RANK, LANES), F32)

        def store(plane, value):
            out_ref[pl.ds(pl.multiple_of(base + plane * RANK, RANK), RANK), :] = value

        block = min(4, PLANES[level])

        def run(first):
            def slot(s, totals):
                totals = list(totals)
                for r in range(RANK):
                    tile_rows = w_ref[pl.ds(pl.multiple_of(s * 1024 + r * RANK, RANK), RANK), :]
                    for p in range(block):
                        at = s * 512 + (first + p) * RANK + r
                        totals[p] = totals[p] + src_ref[pl.ds(at, 1), :] * tile_rows
                return tuple(totals)

            totals = lax.fori_loop(0, 3, slot, tuple(init() for _ in range(block)))
            for p in range(block):
                store(first + p, totals[p])

        if PLANES[level] == block:
            run(0)
        else:
            lax.fori_loop(0, PLANES[level] // block, lambda b, c: (run(b * block), c)[1], 0)


def top_part(par_ref, list_ref, g_ref, e_ref, s_ref, out_ref, m0_ref, m_ref, x_ref, t_ref, w_ref, src_ref, so_t, eo_t):
    d = par_ref[0]
    identity = eye()
    for a in range(4):
        m0_ref[a * LANES : (a + 1) * LANES, :] = g_ref[:, a * LANES : (a + 1) * LANES].T
    for k in range(NK):
        m_ref[k * RANK : (k + 1) * RANK, :] = m0_ref[pl.ds(k, RANK, stride=NK), :]
    transpose_matrices(identity, lambda c: e_ref[0:LANES, c * LANES : (c + 1) * LANES], w_ref)
    known = iota((LANES, LANES), 0) < 120

    def last_rows(c):
        block = e_ref[LANES : 2 * LANES, c * LANES : (c + 1) * LANES].astype(F32)
        return jnp.where(known, block, 0.0).astype(BF16)

    transpose_matrices(identity, last_rows, t_ref)
    row, lane = iota((LANES, 2 * LANES), 0), iota((LANES, 2 * LANES), 1)
    level_of = row >> 4
    own_lane = jnp.where(level_of == 5, 248 + (d >> 5), -1)
    for level in range(5):
        own_lane = jnp.where(level_of == level, 256 - (256 >> level) + (d >> level), own_lane)
    own_rows = ones_where(lane == own_lane)
    filled = iota((2 * LANES, LANES), 0)

    def own_of(ref, rows):
        def rows_of(c):
            block = ref[:, c * LANES : (c + 1) * LANES].astype(F32)
            return dot(own_rows, jnp.where(filled < rows, block, 0.0).astype(BF16)).astype(BF16)

        return rows_of

    for s in range(3):
        transpose_matrices(identity, own_of(s_ref.at[s], 252), so_t, s * 1024)
    transpose_swapped(turn_order(), own_of(e_ref, 248), eo_t)
    for level in range(5):
        if level > 0:
            spread_matrices(level, t_ref, w_ref)
        climb(level, m_ref, START[level], w_ref, x_ref)
        m_ref[START[level + 1] : START[level + 2], :] = pair_sum(level, x_ref)
    row, lane = iota((LANES, LANES), 0), iota((LANES, LANES), 1)
    lane_r = iota((RANK, LANES), 1)
    sources = [jnp.zeros((RANK, LANES), F32) for _ in range(3)]
    for level in range(6):
        planes = PLANES[level]
        high = (lane & (NK - 1)) >> log2(planes)
        delta = row - high * NODES[level]
        here = (lane >> 4) == level
        entries = [list_ref[s, 1024 - (256 >> level) + (d >> level)] for s in range(3)]
        picks = [ones_where(here & (delta == jnp.where(e >= 0, e, -100000))) for e in entries]
        found = dot_exact(m_ref[START[level] : START[level + 1], :], jnp.concatenate(picks, axis=1))
        for plane in range(planes):
            mine = (lane_r & (planes - 1)) == plane
            for s in range(3):
                part = found[plane * RANK : (plane + 1) * RANK, s * LANES : (s + 1) * LANES]
                sources[s] = sources[s] + jnp.where(mine, part, 0.0)
    coupled = jnp.zeros((RANK, LANES), F32)
    for s in range(3):
        src_ref[s * RANK : (s + 1) * RANK, :] = sources[s]
    for s in range(3):
        for r in range(RANK):
            at = s * 1024 + r * RANK
            coupled = coupled + src_ref[s * RANK + r : s * RANK + r + 1, :] * so_t[at : at + RANK, :]
    local = coupled
    for level in reversed(range(5)):
        src_ref[0:RANK, :] = pltpu.roll(local, LANES - NK, 1)
        local = coupled
        for t in range(RANK):
            local = local + src_ref[t : t + 1, :] * eo_t[t * RANK : (t + 1) * RANK, :]
    out_ref[0:RANK, :] = local


def finish_kernel(
    par_ref, list_ref, g_ref, te_ref, ts_ref, four_ref, two_ref, e_any, c0_any, c1_any, ba_any, n0, n1, n2, n3, out_any,
    m0_ref, m_ref, x_ref, tb_ref, w_ref, src_ref, so_t, eo_t, l_ref, p_ref, z_ref, t_ref,
    e_ref, c0_ref, c1_ref, ba_ref, near_ref, out_ref, sems,
):
    copies = [
        pltpu.make_async_copy(source, target, sems.at[j])
        for j, (source, target) in enumerate(
            [(e_any, e_ref), (c1_any, c1_ref), (c0_any, c0_ref), (ba_any, ba_ref)]
            + [(n, near_ref.at[pl.ds(p * PART, PART)]) for p, n in enumerate((n0, n1, n2, n3))]
        )
    ]
    for copy in copies:
        copy.start()
    top_part(par_ref, list_ref, g_ref, te_ref, ts_ref, l_ref, m0_ref, m_ref, x_ref, tb_ref, w_ref, src_ref, so_t, eo_t)
    for copy in copies[:3]:
        copy.wait()
    order = turn_order()
    transpose_swapped(order, tail_rows(e_ref, extra_rows(four_ref, two_ref, par_ref[0])), t_ref)
    for level in reversed(range(LEVELS)):
        if level > 0:
            spread_matrices(level, t_ref, w_ref)
        else:
            transpose_swapped(order, head_rows(e_ref), w_ref)
        given = dot_exact(l_ref[0 : ROWS[level + 1], :], pair_matrix_t(level))
        if level < 4:
            half = ROWS[level + 1]
            p_ref[0:half, :] = given[:, 0:LANES]
            p_ref[half : 2 * half, :] = given[:, LANES : 2 * LANES]
        else:
            p_ref[0:RANK, :] = given

        def row_of(plane, t):
            return p_ref[pl.ds(plane * RANK + t, 1), :]

        def tile_of(t):
            return w_ref[t * RANK : (t + 1) * RANK, :]

        def init(plane):
            if level == 0:
                return c0_ref[plane_rows(plane), :]
            return c1_ref[pl.ds(START[level] - START[1] + plane * RANK, RANK), :]

        def store(plane, value):
            l_ref[plane_rows(plane), :] = value

        contract(PLANES[level], row_of, tile_of, store, init)
    for k in range(NK):
        z_ref[pl.ds(k, LANES, stride=NK), 0:RANK] = l_ref[k * RANK : (k + 1) * RANK, :].T

    for copy in copies[3:]:
        copy.wait()
    sent = []
    for part in range(PARTS):

        def leaf(i, carry):
            at = part * PART + i
            local = z_ref[pl.ds(pl.multiple_of(at * NK, NK), NK), 0:RANK].astype(BF16)
            out_ref[at] = near_ref[at] + dot(local, ba_ref[at])
            return carry

        lax.fori_loop(0, PART, leaf, 0, unroll=16)
        rows = pl.ds(part * PART, PART)
        sent.append(pltpu.make_async_copy(out_ref.at[rows], out_any.at[rows], sems.at[8 + part]))
        sent[-1].start()
    for copy in sent:
        copy.wait()


def three(x):
    first = x.astype(BF16).astype(F32)
    rest = x - first
    second = rest.astype(BF16).astype(F32)
    return first, second, (rest - second).astype(BF16).astype(F32)


def near_kernel(part, *refs):
    par_ref, list_ref, pt_ref, ch_ref, ptl_ref, chl_ref, ptr_ref, chr_ref = refs[:8]
    out_ref, fa_ref, fs_ref, fn_ref, k_ref = refs[-5:]
    d = par_ref[0]
    odd = (d & 1) == 1
    first_leaf = part * PART
    base = d * LANES + first_leaf
    left = [ptl_ref[c, 7:8, :] for c in range(3)]
    right = [ptr_ref[c, 0:1, :] for c in range(3)]
    left_charges, right_charges = chl_ref[0], chr_ref[0]
    if len(refs) > 13:
        near_msg, far_msg = refs[8:10]
        if part == 0:
            halo = jnp.where(odd, near_msg[...], far_msg[...])
            left = [halo[c : c + 1, :] for c in range(3)]
            left_charges = halo[8:24, :].astype(BF16)
        else:
            halo = jnp.where(odd, far_msg[...], near_msg[...])
            right = [halo[c : c + 1, :] for c in range(3)]
            right_charges = halo[8:24, :].astype(BF16)
    soft = jnp.float32(SOFTENING) * (SCALE * SCALE)
    row8 = iota((FRAME, LANES), 0) & 7
    fa_ref[...] = jnp.where(row8 == 4, 1.0, 0.0)
    fs_ref[...] = jnp.where(row8 == 3, 1.0, 0.0)
    fn_ref[...] = jnp.where(row8 == 3, 1.0, 0.0)

    def features(values, first_leaf, put):
        x = ((values[0] - first_leaf.astype(F32)) - 0.5) * SCALE
        y, z = (values[1] - 0.5) * SCALE, (values[2] - 0.5) * SCALE
        moved = x + SCALE
        flat = y * y + z * z
        for j, value in enumerate((x, y, z, x * x + flat)):
            put(fa_ref, j, value)
        for ref, along in ((fs_ref, x), (fn_ref, moved)):
            for j, value in ((0, -2.0 * along), (1, -2.0 * y), (2, -2.0 * z), (4, along * along + flat + soft)):
                put(ref, j, value)

    def put_own(ref, j, value):
        ref[pl.ds(8 + j, PART, stride=8), :] = value

    def put_left(ref, j, value):
        ref[j : j + 1, :] = value

    def put_right(ref, j, value):
        at = (PART + 1) * 8 + j
        ref[at : at + 1, :] = value

    features([pt_ref[0], pt_ref[1], pt_ref[2]], iota((PART, LANES), 0) + base, put_own)
    one_leaf = iota((1, LANES), 0) + base
    features(left, one_leaf - 1, put_left)
    features(right, one_leaf + PART, put_right)

    def lists(i, offset):
        wanted = base + i + offset
        at = first_leaf + i
        hit = (list_ref[0, at] == wanted) | (list_ref[1, at] == wanted) | (list_ref[2, at] == wanted)
        return jnp.where(hit, 1.0, 0.0).astype(F32)

    def pieces(ref, w):
        return three(ref[pl.ds(pl.multiple_of(w * 8, 8), 8), :])

    def source_of(w):
        a, b, c = pieces(fa_ref, w)
        return jnp.concatenate([a, a, b, b, a, c], axis=0).astype(BF16)

    def target_of(ref, w):
        a, b, c = pieces(ref, w)
        return jnp.concatenate([a, b, a, b, c, a], axis=0).astype(BF16)

    def kernel_of(source, target):
        return lax.rsqrt(dot_tn(source, target)).astype(BF16)

    first = dot(left_charges, kernel_of(source_of(0), target_of(fn_ref, 1)))

    def fill(i, carry):
        both = jnp.concatenate([target_of(fs_ref, i + 1), target_of(fn_ref, i + 2)], axis=1)
        k_ref[i] = kernel_of(source_of(i + 1), both)
        return carry


    def step(i, carry, own, after):
        spread = dot(own, k_ref[i])
        back = dot_nt(after, k_ref[i, :, LANES : 2 * LANES])
        out_ref[i] = carry + spread[:, 0:LANES] + lists(i, 1) * back
        return spread[:, LANES : 2 * LANES]

    def body(i, carry):
        onward = step(i, carry, ch_ref[i], ch_ref[i + 1])
        return lists(i + 1, -1) * onward

    carry = lists(0, -1) * first
    for i in range(AHEAD):
        fill(i, 0)
    for i in range(PART - 1):
        if i + AHEAD < PART:
            fill(i + AHEAD, 0)
        carry = body(i, carry)
    step(PART - 1, carry, ch_ref[PART - 1], right_charges)


VMEM = pl.BlockSpec(memory_space=pltpu.VMEM)
SMEM = pl.BlockSpec(memory_space=pltpu.SMEM)
ANY = pl.BlockSpec(memory_space=pl.ANY)


def scratch(*shape, dtype=F32):
    return pltpu.VMEM(shape, dtype)


def shape(*dims):
    return jax.ShapeDtypeStruct(dims, F32)


def whole(*dims):
    return pl.BlockSpec(dims, lambda i, par: (0,) * len(dims))


NEAR_SCRATCH = [scratch(FRAME, LANES)] * 3 + [scratch(PART, LANES, 2 * LANES, dtype=BF16)]
FOUR = pl.BlockSpec((8, 1024), lambda i, par: (par[0] >> 1, 0))
TWO = pl.BlockSpec((8, 1024), lambda i, par: (64 + (par[0] >> 2), 0))
FOUR_C = pl.BlockSpec((3, 8, 1024), lambda i, par: (0, par[0] >> 1, 0))
TWO_C = pl.BlockSpec((3, 8, 1024), lambda i, par: (0, 64 + (par[0] >> 2), 0))
LEAF_SPEC = pl.BlockSpec((HEAD, LANES), lambda i, par: (0, 0))


def call(kernel, in_specs, out_specs, out_shape, scratch_shapes):
    return pl.pallas_call(
        kernel,
        grid_spec=pltpu.PrefetchScalarGridSpec(
            num_scalar_prefetch=1,
            grid=(1,),
            in_specs=in_specs,
            out_specs=out_specs,
            scratch_shapes=scratch_shapes,
        ),
        out_shape=out_shape,
    )


def hop_partner(device, bit):
    if bit == 0 or bit & 1:
        return device ^ (1 << bit)
    low = bit - 1
    place = (device >> low) & 3
    other = (place + 1) & 3 if place & 1 else (place - 1) & 3
    return device + ((other - place) << low)


def on_device(
    charges, points, basis, near_list, loc_coupling, loc_transfer, loc_lists, top_coupling, top_transfer, top_lists
):
    devices = lax.axis_size("cluster")
    d = lax.axis_index("cluster")
    mates = [(i, i ^ 1) for i in range(devices)]
    others = [(i, ((i + 1) ^ 1) - 1) for i in range(devices) if 0 <= ((i + 1) ^ 1) - 1 < devices]
    par = d.astype(jnp.int32).reshape(1)
    points_t = jnp.transpose(points, (1, 0, 2))
    transfer = loc_transfer[0]
    coupling = jnp.transpose(loc_coupling[0], (1, 0, 2))
    top_c = jnp.transpose(top_coupling, (1, 0, 2))
    top_l = jnp.transpose(top_lists)
    message = HEAD + ROWS[0]
    moments, msg_near, msg_far, device_moment = call(
        up_kernel,
        [whole(LANES, NK, LANES), whole(3, LANES, LANES), whole(LANES, RANK, LANES), whole(248, 1024), FOUR, TWO],
        [whole(M_ROWS, LANES), whole(message, LANES), whole(message, LANES), whole(1, 512)],
        [shape(M_ROWS, LANES), shape(message, LANES), shape(message, LANES), shape(1, 512)],
        [scratch(2048, LANES), scratch(512, LANES), scratch(1024, LANES, dtype=BF16), scratch(1024, LANES)],
    )(par, charges, points_t, basis, transfer, top_transfer, top_transfer)

    halo_near = lax.ppermute(msg_near, "cluster", mates)
    halo_far = lax.ppermute(msg_far, "cluster", others)
    gathered = device_moment
    for bit in range(7):
        partner = lax.ppermute(gathered, "cluster", [(i, hop_partner(i, bit)) for i in range(devices)])
        upper = ((d >> bit) & 1) == 1
        gathered = jnp.concatenate(
            [jnp.where(upper, partner, gathered), jnp.where(upper, gathered, partner)], axis=0
        )

    near_list_t = near_list.T
    near = []
    for part in range(PARTS):
        lower, upper_leaf = max(PART * part - 1, 0), min(PART * (part + 1), LANES - 1)
        specs = [
            SMEM,
            pl.BlockSpec((3, PART, LANES), lambda i, par, p=part: (0, p, 0)),
            pl.BlockSpec((PART, NK, LANES), lambda i, par, p=part: (p, 0, 0)),
            pl.BlockSpec((3, 8, LANES), lambda i, par, p=lower: (0, p // 8, 0)),
            pl.BlockSpec((1, NK, LANES), lambda i, par, p=lower: (p, 0, 0)),
            pl.BlockSpec((3, 8, LANES), lambda i, par, p=upper_leaf: (0, p // 8, 0)),
            pl.BlockSpec((1, NK, LANES), lambda i, par, p=upper_leaf: (p, 0, 0)),
        ]
        operands = [near_list_t, points_t, charges, points_t, charges, points_t, charges]
        if part in (0, PARTS - 1):
            specs += [LEAF_SPEC, LEAF_SPEC]
            operands += [halo_near, halo_far]
        near.append(
            call(
                functools.partial(near_kernel, part),
                specs,
                whole(PART, NK, LANES),
                shape(PART, NK, LANES),
                NEAR_SCRATCH,
            )(par, *operands)
        )

    coupled = []
    fine_lists = jnp.transpose(loc_lists, (2, 0, 1))
    for levels in ((0,), tuple(range(1, LEVELS))):
        out_rows = sum(ROWS[level] for level in levels)
        coupled.append(
            call(
                functools.partial(couple_kernel, levels),
                [
                    whole(M_ROWS, LANES),
                    whole(message, LANES),
                    whole(message, LANES),
                    whole(3, 1, 248),
                    SMEM,
                    whole(3, 248, 1024),
                    FOUR_C,
                    TWO_C,
                ],
                whole(out_rows, LANES),
                shape(out_rows, LANES),
                [scratch(1536, LANES), scratch(3072, LANES, dtype=BF16), scratch(3072, LANES), scratch(8, 2 * LANES)],
            )(par, moments, halo_near, halo_far, fine_lists, top_l, coupling, top_c, top_c)
        )

    return call(
        finish_kernel,
        [
            SMEM,
            whole(LANES, 512),
            pl.BlockSpec((256, 1024), lambda i, par: (3, 0)),
            pl.BlockSpec((3, 256, 1024), lambda i, par: (0, 3, 0)),
            FOUR,
            TWO,
        ]
        + [ANY] * (4 + PARTS),
        ANY,
        shape(LANES, NK, LANES),
        [
            scratch(512, LANES),
            scratch(START[6], LANES),
            scratch(512, LANES),
            scratch(1024, LANES, dtype=BF16),
            scratch(1024, LANES),
            scratch(96, LANES),
            scratch(3072, LANES),
            scratch(1024, LANES),
            scratch(512, LANES),
            scratch(512, LANES),
            scratch(2048, LANES),
            scratch(1024, LANES),
            scratch(248, 1024, dtype=BF16),
            scratch(ROWS[0], LANES),
            scratch(M_ROWS - ROWS[0], LANES),
            scratch(LANES, RANK, LANES, dtype=BF16),
            scratch(LANES, NK, LANES),
            scratch(LANES, NK, LANES),
            pltpu.SemaphoreType.DMA((8 + PARTS,)),
        ],
    )(par, top_l, gathered, top_transfer, top_c, top_transfer, top_transfer, transfer, *coupled, basis, *near)


def solution(mesh):
    placed = (
        P("cluster", None, None),
        P("cluster", None, None),
        P("cluster", None, None),
        P("cluster", None),
        P("cluster", None, None, None),
        P("cluster", None, None),
        P("cluster", None, None),
        P(),
        P(),
        P(),
    )
    return jax.shard_map(on_device, mesh=mesh, in_specs=placed, out_specs=P("cluster", None, None), check_vma=False)
```

```python
import functools

import jax
import jax.numpy as jnp
from jax import lax
from jax.experimental import pallas as pl
from jax.experimental.pallas import tpu as pltpu
from jax.sharding import PartitionSpec as P


AREA_WEIGHT = 0.0625
SOFTENING = 0.0025
SCALE = 1.0 / AREA_WEIGHT

NK = 16
RANK = 32
LANES = 128
LEVELS = 7
F32 = jnp.float32
BF16 = jnp.bfloat16

NODES = [LANES >> level for level in range(8)]
FOLD = [min(NK, 1 << level) for level in range(8)]
PLANES = [NK // fold for fold in FOLD]
ROWS = [planes * RANK for planes in PLANES]
START = [sum(ROWS[:level]) for level in range(9)]
TILE_ROW = [0, 0, 64, 96, 112, 120, 124, 126]
HALO_LANE = [0, 2, 6, 14, 30, 62, 94]
BASE = START[:6] + [START[5]]
M_ROWS = START[6]
SHARED = LANES // 2
HEAD = 24
PART = 32
PARTS = LANES // PART
AHEAD = 8
FRAME = 8 * (PART + 2)


def log2(value):
    return value.bit_length() - 1


def iota(shape, dim):
    return lax.broadcasted_iota(jnp.int32, shape, dim)


def ones_where(cond):
    return jnp.where(cond, 1.0, 0.0).astype(BF16)


def dot(a, b):
    return jnp.dot(a, b, preferred_element_type=F32)


def dot_nt(a, b):
    return lax.dot_general(a, b, (((1,), (1,)), ((), ())), preferred_element_type=F32)


def dot_tn(a, b):
    return lax.dot_general(a, b, (((0,), (0,)), ((), ())), preferred_element_type=F32)


def split(x):
    high = x.astype(BF16)
    low = (x - high.astype(F32)).astype(BF16)
    return high, low


def dot_exact(x, selection):
    high, low = split(x)
    return dot(high, selection) + dot(low, selection)


def eye():
    return ones_where(iota((LANES, LANES), 0) == iota((LANES, LANES), 1))


def pair_target(level, index):
    nodes = NODES[level]
    lane = index & (LANES - 1)
    node = lane & (nodes - 1)
    high = lane >> log2(nodes)
    if level < 4:
        half = index >> 7
        return high * nodes + half * (nodes // 2) + (node >> 1)
    if level == 6:
        return jnp.where((lane >= SHARED) & (lane < SHARED + 2 * NK), (lane - SHARED) >> 1, -1)
    target = high * (nodes // 2) + (node >> 1)
    return jnp.where(lane < NK * nodes, target + (SHARED if level == 5 else 0), -1)


def pair_matrix(level):
    depth = 2 * LANES if level < 4 else LANES
    return ones_where(pair_target(level, iota((depth, LANES), 0)) == iota((depth, LANES), 1))


def pair_matrix_t(level):
    width = 2 * LANES if level < 4 else LANES
    return ones_where(pair_target(level, iota((LANES, width), 1)) == iota((LANES, width), 0))


def spread_matrix(level):
    nodes = NODES[level]
    row, lane = iota((LANES, LANES), 0), iota((LANES, LANES), 1)
    if level == 5:
        wanted = jnp.where(lane < SHARED, TILE_ROW[5] + (lane & 3), TILE_ROW[6] + (lane & 1))
        return ones_where((row == wanted) & (lane < SHARED + 2 * NK))
    return ones_where((row == TILE_ROW[level] + (lane & (nodes - 1))) & (lane < FOLD[level] * nodes))


def turn_order():
    row, lane = iota((2 * LANES, 2 * LANES), 0), iota((2 * LANES, 2 * LANES), 1)
    return ones_where(row == (lane & (RANK - 1)) * 8 + (lane >> 5))


def transpose_swapped(order, rows_of, out_ref):
    for pair in range(4):
        turned = dot_nt(order, jnp.concatenate([rows_of(2 * pair), rows_of(2 * pair + 1)], axis=1))
        for t in range(RANK):
            out_ref[t * RANK + 8 * pair : t * RANK + 8 * pair + 8, :] = turned[8 * t : 8 * t + 8, :]


def extra_rows(four_ref, two_ref, d):
    four = pltpu.roll(four_ref[...].astype(F32), (8 - 4 * (d & 1)) & 7, 0)
    two = pltpu.roll(two_ref[...].astype(F32), (12 - 2 * (d & 3)) & 7, 0)
    row = iota((8, 1024), 0)
    return jnp.where(row < 4, four, jnp.where(row < 6, two, 0.0))


def head_rows(ref):
    return lambda c: ref[0:LANES, c * LANES : (c + 1) * LANES]


def tail_rows(ref, extra, first=LANES):
    def rows_of(c):
        cut = slice(c * LANES, (c + 1) * LANES)
        return jnp.concatenate([ref[first : first + 120, cut].astype(F32), extra[:, cut]], axis=0).astype(BF16)

    return rows_of


def transpose_matrices(identity, rows_of, out_ref, base=0):
    for chunk in range(8):
        turned = dot_nt(identity, rows_of(chunk))
        out_ref[base + chunk * LANES : base + (chunk + 1) * LANES, :] = turned.astype(out_ref.dtype)


def spread_matrices(level, turned_ref, out_ref, base=0):
    spread = spread_matrix(level)
    for chunk in range(8):
        rows = slice(base + chunk * LANES, base + (chunk + 1) * LANES)
        out_ref[rows, :] = dot(turned_ref[rows, :].astype(BF16), spread)


def contract(plane_count, row_of, tile_of, store, init=None):
    block = min(4, plane_count)

    def run(first):
        if init is None:
            totals = [jnp.zeros((RANK, LANES), F32) for _ in range(block)]
        else:
            totals = [init(first + p) for p in range(block)]
        for r in range(RANK):
            tile = tile_of(r)
            for p in range(block):
                totals[p] = totals[p] + row_of(first + p, r) * tile
        for p in range(block):
            store(first + p, totals[p])

    if plane_count == block:
        run(0)
    else:
        lax.fori_loop(0, plane_count // block, lambda b, c: (run(b * block), c)[1], 0)


def plane_rows(plane):
    if isinstance(plane, int):
        return slice(plane * RANK, (plane + 1) * RANK)
    return pl.ds(pl.multiple_of(plane * RANK, RANK), RANK)


def climb(level, m_ref, source_base, matrix_ref, x_ref):
    def row_of(plane, r):
        return m_ref[pl.ds(source_base + plane * RANK + r, 1), :]

    def tile_of(r):
        return matrix_ref[r * RANK : (r + 1) * RANK, :]

    def store(plane, value):
        x_ref[plane_rows(plane), :] = value

    contract(PLANES[level], row_of, tile_of, store)


def pair_sum(level, x_ref):
    if level < 4:
        half = ROWS[level] // 2
        x = jnp.concatenate([x_ref[0:half, :], x_ref[half : 2 * half, :]], axis=1)
    else:
        x = x_ref[0:RANK, :]
    return dot_exact(x, pair_matrix(level))


def up_kernel(
    par_ref, ch_ref, pt_ref, ba_any, e_any, four_ref, two_ref, m_ref, near_msg, far_msg, top_ref,
    y_ref, x_ref, t_ref, w_ref, ba_ref, e_ref, sems,
):
    parts = [pl.ds(p * PART, PART) for p in range(PARTS)]
    copies = [pltpu.make_async_copy(ba_any.at[p], ba_ref.at[p], sems.at[j]) for j, p in enumerate(parts)]
    copies.append(pltpu.make_async_copy(e_any, e_ref, sems.at[PARTS]))
    for copy in copies:
        copy.start()
    d = par_ref[0]
    odd = d & 1
    first_leaf = [pt_ref[:, 0, :], ch_ref[0].astype(F32)]
    last_leaf = [pt_ref[:, LANES - 1, :], ch_ref[LANES - 1].astype(F32)]
    near_msg[0:HEAD, :] = jnp.zeros((HEAD, LANES), F32)
    far_msg[0:HEAD, :] = jnp.zeros((HEAD, LANES), F32)
    for rows, first, last in zip((slice(0, 3), slice(8, 24)), first_leaf, last_leaf):
        near_msg[rows, :] = jnp.where(odd == 1, first, last)
        far_msg[rows, :] = jnp.where(odd == 1, last, first)

    def leaf(i, carry):
        y_ref[pl.ds(pl.multiple_of(i * NK, NK), NK), 0:RANK] = dot_nt(ch_ref[i], ba_ref[i])
        return carry

    for part in range(PARTS):
        copies[part].wait()
        lax.fori_loop(part * PART, (part + 1) * PART, leaf, 0, unroll=16)
    copies[PARTS].wait()
    identity = eye()
    transpose_matrices(identity, head_rows(e_ref), w_ref)
    transpose_matrices(identity, tail_rows(e_ref, extra_rows(four_ref, two_ref, d)), t_ref)
    for k in range(NK):
        m_ref[k * RANK : (k + 1) * RANK, :] = y_ref[pl.ds(k, LANES, stride=NK), :].T[0:RANK, :]
    for level in range(LEVELS):
        if 0 < level < 6:
            spread_matrices(level, t_ref, w_ref)
        climb(level, m_ref, BASE[level], w_ref, x_ref)
        if level < 5:
            m_ref[START[level + 1] : START[level + 2], :] = pair_sum(level, x_ref)
        elif level == 5:
            m_ref[BASE[6] : M_ROWS, :] += pair_sum(level, x_ref)
    row, lane = iota((LANES, LANES), 0), iota((LANES, LANES), 1)
    spread = ones_where(((row - SHARED) >> 1 == (lane & (NK - 1))) & (row >= SHARED) & (row < SHARED + 2 * NK))
    device = dot_exact(x_ref[0:RANK, :], spread)
    sub, lane8 = iota((8, LANES), 0), iota((8, LANES), 1)
    for a in range(4):
        kept = jnp.where(sub == (lane8 >> 4), device[8 * a : 8 * a + 8, :], 0.0)
        top_ref[:, a * LANES : (a + 1) * LANES] = jnp.sum(kept, axis=0, keepdims=True)
    row, lane = iota((LANES, 2 * LANES), 0), iota((LANES, 2 * LANES), 1)
    first = odd ^ (lane >> 7)

    def wanted_nodes(level):
        nodes = NODES[level]
        slot = (lane & (LANES - 1)) - HALO_LANE[level]
        node = (slot & 1) + jnp.where(first == 1, 0, nodes - 2)
        wanted = (slot >> 1) * nodes + node + (SHARED if level == 6 else 0)
        return (slot >= 0) & (slot < 2 * FOLD[level]) & (row == wanted)

    near_msg[HEAD:, :] = jnp.zeros((ROWS[0], LANES), F32)
    far_msg[HEAD:, :] = jnp.zeros((ROWS[0], LANES), F32)
    for level in range(6):
        wanted = wanted_nodes(level)
        if level == 5:
            wanted = wanted | wanted_nodes(6)
        picked = dot_exact(m_ref[START[level] : START[level + 1], :], ones_where(wanted))
        near_msg[HEAD : HEAD + ROWS[level], :] += picked[:, 0:LANES]
        far_msg[HEAD : HEAD + ROWS[level], :] += picked[:, LANES : 2 * LANES]


def couple_kernel(
    levels,
    par_ref, m_ref, near_ref, far_ref, list_ref, top_list, s_ref, four_ref, two_ref, out_ref, src_ref, t_ref, w_ref, rel_ref
):
    d = par_ref[0]
    odd = (d & 1) == 1
    place = iota((1, LANES), 1)
    rel_ref[...] = jnp.full((8, 2 * LANES), 64.0, F32)
    start = jnp.where(place < 64, 0, jnp.where(place < 96, 64, jnp.where(place < 112, 96, 112)))
    count = jnp.where(place < 64, 64, jnp.where(place < 96, 32, jnp.where(place < 112, 16, 8)))
    for s in range(3):
        fine = list_ref[s, :, 0:LANES]
        rel_ref[s : s + 1, 0:LANES] = jnp.where(fine >= 0, fine - (d * LANES + place), 64).astype(F32)
        rest = list_ref[s, :, LANES:248]
        own = (d * count + place - start)[:, 0:120]
        rel_ref[s : s + 1, LANES:248] = jnp.where(rest >= 0, rest - own, 64).astype(F32)
        row = rel_ref[s : s + 1, LANES : 2 * LANES]
        for lane_at, base, nodes in ((120, 4 * d, 4), (124, 512 + 2 * d, 2)):
            for t in range(nodes):
                entry = top_list[s, base + t]
                index = (4 * d if nodes == 4 else 2 * d) + t
                value = jnp.where(entry >= 0, entry - index, 64).astype(F32)
                row = jnp.where(place == lane_at + t, value, row)
        rel_ref[s : s + 1, LANES : 2 * LANES] = row
    identity = eye()
    row = iota((LANES, LANES), 0)
    lane = iota((1, LANES), 1)
    shift_rows = START[levels[0]]
    if levels[0] > 0:
        for s in range(3):
            extra = extra_rows(four_ref.at[s], two_ref.at[s], d)
            transpose_matrices(identity, tail_rows(s_ref.at[s], extra, 0), t_ref, s * 1024)
    for level in levels:
        nodes, rows = NODES[level], ROWS[level]
        tile = 0 if level == 0 else 1
        for s in range(3):
            if level == 0:
                transpose_matrices(identity, head_rows(s_ref.at[s]), w_ref, s * 1024)
            else:
                spread_matrices(level, t_ref, w_ref, s * 1024)
        rel = rel_ref[:, tile * LANES : (tile + 1) * LANES]
        if level > 0:
            rel = dot(rel.astype(BF16), spread_matrix(level))
        rel = rel.astype(jnp.int32)
        moments = m_ref[START[level] - shift_rows : START[level + 1] - shift_rows, :]
        near_part, far_part = near_ref[HEAD : HEAD + rows, :], far_ref[HEAD : HEAD + rows, :]
        left = split(jnp.where(odd, near_part, far_part))
        right = split(jnp.where(odd, far_part, near_part))
        own = split(moments)
        halo_lane, start_lane, place = HALO_LANE[level], 0, lane
        high = lane >> log2(nodes)
        if level == 5:
            low = lane < SHARED
            nodes = jnp.where(low, 4, 2)
            halo_lane, start_lane = jnp.where(low, HALO_LANE[5], HALO_LANE[6]), jnp.where(low, 0, SHARED)
            place = lane - start_lane
            high = jnp.where(low, place >> 2, place >> 1)
        node = place & (nodes - 1)
        for s in range(3):
            shift = rel[s : s + 1, :]
            target = node + shift
            usable = (shift >= -3) & (shift <= 3)
            inside = usable & (target >= 0) & (target < nodes)
            at_own = jnp.where(inside, start_lane + high * nodes + target, -1)
            at_left = jnp.where(usable & (target < 0), halo_lane + 2 * high + target + 2, -1)
            at_right = jnp.where(usable & (target >= nodes), halo_lane + 2 * high + target - nodes, -1)
            total = None
            for part, at in ((own, at_own), (left, at_left), (right, at_right)):
                pick = ones_where(row == at)
                piece = dot(part[0], pick) + dot(part[1], pick)
                total = piece if total is None else total + piece
            src_ref[s * 512 : s * 512 + rows, :] = total

        base = START[level] - shift_rows

        def init():
            return jnp.zeros((RANK, LANES), F32)

        def store(plane, value):
            out_ref[pl.ds(pl.multiple_of(base + plane * RANK, RANK), RANK), :] = value

        block = min(4, PLANES[level])

        def run(first):
            def slot(s, totals):
                totals = list(totals)
                for r in range(RANK):
                    tile_rows = w_ref[pl.ds(pl.multiple_of(s * 1024 + r * RANK, RANK), RANK), :]
                    for p in range(block):
                        at = s * 512 + (first + p) * RANK + r
                        totals[p] = totals[p] + src_ref[pl.ds(at, 1), :] * tile_rows
                return tuple(totals)

            totals = lax.fori_loop(0, 3, slot, tuple(init() for _ in range(block)))
            for p in range(block):
                store(first + p, totals[p])

        if PLANES[level] == block:
            run(0)
        else:
            lax.fori_loop(0, PLANES[level] // block, lambda b, c: (run(b * block), c)[1], 0)


def top_part(par_ref, list_ref, own_ref, partner_ref, e_ref, s_refs, out_ref, m0_ref, m_ref, x_ref, t_ref, w_ref, src_ref, so_t, eo_t):
    d = par_ref[0]
    identity = eye()
    upper = (d >> 6) == 1
    for a in range(4):
        cut = slice(a * LANES, (a + 1) * LANES)
        own, partner = own_ref[:, cut], partner_ref[:, cut]
        both = [jnp.where(upper, partner, own), jnp.where(upper, own, partner)]
        m0_ref[cut, :] = jnp.concatenate(both, axis=0).T
    for k in range(NK):
        m_ref[k * RANK : (k + 1) * RANK, :] = m0_ref[pl.ds(k, RANK, stride=NK), :]
    transpose_matrices(identity, lambda c: e_ref[0:LANES, c * LANES : (c + 1) * LANES], w_ref)
    known = iota((LANES, LANES), 0) < 120

    def last_rows(c):
        block = e_ref[LANES : 2 * LANES, c * LANES : (c + 1) * LANES].astype(F32)
        return jnp.where(known, block, 0.0).astype(BF16)

    transpose_matrices(identity, last_rows, t_ref)
    row, lane = iota((LANES, 2 * LANES), 0), iota((LANES, 2 * LANES), 1)
    level_of = row >> 4
    own_lane = jnp.where(level_of == 5, 248 + (d >> 5), -1)
    for level in range(5):
        own_lane = jnp.where(level_of == level, 256 - (256 >> level) + (d >> level), own_lane)
    own_rows = ones_where(lane == own_lane)
    filled = iota((2 * LANES, LANES), 0)

    def own_transfer(c):
        block = e_ref[:, c * LANES : (c + 1) * LANES].astype(F32)
        return dot(own_rows, jnp.where(filled < 248, block, 0.0).astype(BF16)).astype(BF16)

    row48, lane48 = iota((LANES, 48), 0) >> 4, iota((LANES, 48), 1)
    own_lane48 = jnp.zeros((LANES, 48), jnp.int32)
    for level in range(6):
        own_lane48 = jnp.where(row48 == level, 8 * level + ((d >> level) & 7), own_lane48)
    own_rows48 = ones_where((lane48 == own_lane48) & (row48 < 6))
    known8 = iota((8, LANES), 0) < 4

    def own_coupling(s):
        def rows_of(c):
            pieces = [ref[s, :, c * LANES : (c + 1) * LANES].astype(F32) for ref in s_refs]
            pieces[5] = jnp.where(known8, pieces[5], 0.0)
            return dot(own_rows48, jnp.concatenate(pieces, axis=0).astype(BF16)).astype(BF16)

        return rows_of

    for s in range(3):
        transpose_matrices(identity, own_coupling(s), so_t, s * 1024)
    transpose_swapped(turn_order(), own_transfer, eo_t)
    for level in range(5):
        if level > 0:
            spread_matrices(level, t_ref, w_ref)
        climb(level, m_ref, START[level], w_ref, x_ref)
        m_ref[START[level + 1] : START[level + 2], :] = pair_sum(level, x_ref)
    row, lane = iota((LANES, LANES), 0), iota((LANES, LANES), 1)
    lane_r = iota((RANK, LANES), 1)
    sources = [jnp.zeros((RANK, LANES), F32) for _ in range(3)]
    for level in range(6):
        planes = PLANES[level]
        high = (lane & (NK - 1)) >> log2(planes)
        delta = row - high * NODES[level]
        here = (lane >> 4) == level
        entries = [list_ref[s, 1024 - (256 >> level) + (d >> level)] for s in range(3)]
        picks = [ones_where(here & (delta == jnp.where(e >= 0, e, -100000))) for e in entries]
        found = dot_exact(m_ref[START[level] : START[level + 1], :], jnp.concatenate(picks, axis=1))
        for plane in range(planes):
            mine = (lane_r & (planes - 1)) == plane
            for s in range(3):
                part = found[plane * RANK : (plane + 1) * RANK, s * LANES : (s + 1) * LANES]
                sources[s] = sources[s] + jnp.where(mine, part, 0.0)
    coupled = jnp.zeros((RANK, LANES), F32)
    for s in range(3):
        src_ref[s * RANK : (s + 1) * RANK, :] = sources[s]
    for s in range(3):
        for r in range(RANK):
            at = s * 1024 + r * RANK
            coupled = coupled + src_ref[s * RANK + r : s * RANK + r + 1, :] * so_t[at : at + RANK, :]
    local = coupled
    for level in reversed(range(5)):
        src_ref[0:RANK, :] = pltpu.roll(local, LANES - NK, 1)
        local = coupled
        for t in range(RANK):
            local = local + src_ref[t : t + 1, :] * eo_t[t * RANK : (t + 1) * RANK, :]
    out_ref[0:RANK, :] = local


def finish_kernel(
    par_ref, list_ref, own_ref, partner_ref, te_ref, ts0, ts1, ts2, ts3, ts4, ts5, four_ref, two_ref, e_any, c0_any, c1_any, ba_any, n0, n1, n2, n3, out_any,
    m0_ref, m_ref, x_ref, tb_ref, w_ref, src_ref, so_t, eo_t, l_ref, p_ref, z_ref, t_ref,
    e_ref, c0_ref, c1_ref, ba_ref, near_ref, out_ref, sems,
):
    copies = [
        pltpu.make_async_copy(source, target, sems.at[j])
        for j, (source, target) in enumerate(
            [(e_any, e_ref), (c1_any, c1_ref), (c0_any, c0_ref), (ba_any, ba_ref)]
            + [(n, near_ref.at[pl.ds(p * PART, PART)]) for p, n in enumerate((n0, n1, n2, n3))]
        )
    ]
    for copy in copies:
        copy.start()
    s_refs = (ts0, ts1, ts2, ts3, ts4, ts5)
    top_part(par_ref, list_ref, own_ref, partner_ref, te_ref, s_refs, l_ref, m0_ref, m_ref, x_ref, tb_ref, w_ref, src_ref, so_t, eo_t)
    for copy in copies[:3]:
        copy.wait()
    order = turn_order()
    transpose_swapped(order, tail_rows(e_ref, extra_rows(four_ref, two_ref, par_ref[0])), t_ref)
    for level in reversed(range(LEVELS)):
        if level == 6:
            spread_matrices(5, t_ref, w_ref)
        elif 0 < level < 5:
            spread_matrices(level, t_ref, w_ref)
        elif level == 0:
            transpose_swapped(order, head_rows(e_ref), w_ref)
        given = dot_exact(l_ref[0 : ROWS[level + 1], :], pair_matrix_t(level))
        if level < 4:
            half = ROWS[level + 1]
            p_ref[0:half, :] = given[:, 0:LANES]
            p_ref[half : 2 * half, :] = given[:, LANES : 2 * LANES]
        else:
            p_ref[0:RANK, :] = given

        def row_of(plane, t):
            return p_ref[pl.ds(plane * RANK + t, 1), :]

        def tile_of(t):
            return w_ref[t * RANK : (t + 1) * RANK, :]

        def init(plane):
            if level == 0:
                return c0_ref[plane_rows(plane), :]
            return c1_ref[pl.ds(BASE[level] - START[1] + plane * RANK, RANK), :]

        def store(plane, value):
            l_ref[plane_rows(plane), :] = value

        contract(PLANES[level], row_of, tile_of, store, init)
    for k in range(NK):
        z_ref[pl.ds(k, LANES, stride=NK), 0:RANK] = l_ref[k * RANK : (k + 1) * RANK, :].T

    for copy in copies[3:]:
        copy.wait()
    sent = []
    for part in range(PARTS):

        def leaf(i, carry):
            at = part * PART + i
            local = z_ref[pl.ds(pl.multiple_of(at * NK, NK), NK), 0:RANK].astype(BF16)
            out_ref[at] = near_ref[at] + dot(local, ba_ref[at])
            return carry

        lax.fori_loop(0, PART, leaf, 0, unroll=16)
        rows = pl.ds(part * PART, PART)
        sent.append(pltpu.make_async_copy(out_ref.at[rows], out_any.at[rows], sems.at[8 + part]))
        sent[-1].start()
    for copy in sent:
        copy.wait()


def three(x):
    first = x.astype(BF16).astype(F32)
    rest = x - first
    second = rest.astype(BF16).astype(F32)
    return first, second, (rest - second).astype(BF16).astype(F32)


def near_kernel(part, *refs):
    par_ref, list_ref, pt_ref, ch_ref, ptl_ref, chl_ref, ptr_ref, chr_ref = refs[:8]
    out_ref, fa_ref, fs_ref, fn_ref, k_ref = refs[-5:]
    d = par_ref[0]
    odd = (d & 1) == 1
    first_leaf = part * PART
    base = d * LANES + first_leaf
    left = [ptl_ref[c, 7:8, :] for c in range(3)]
    right = [ptr_ref[c, 0:1, :] for c in range(3)]
    left_charges, right_charges = chl_ref[0], chr_ref[0]
    if len(refs) > 13:
        near_msg, far_msg = refs[8:10]
        if part == 0:
            halo = jnp.where(odd, near_msg[0:HEAD, :], far_msg[0:HEAD, :])
            left = [halo[c : c + 1, :] for c in range(3)]
            left_charges = halo[8:24, :].astype(BF16)
        else:
            halo = jnp.where(odd, far_msg[0:HEAD, :], near_msg[0:HEAD, :])
            right = [halo[c : c + 1, :] for c in range(3)]
            right_charges = halo[8:24, :].astype(BF16)
    soft = jnp.float32(SOFTENING) * (SCALE * SCALE)
    row8 = iota((FRAME, LANES), 0) & 7
    fa_ref[...] = jnp.where(row8 == 4, 1.0, 0.0)
    fs_ref[...] = jnp.where(row8 == 3, 1.0, 0.0)
    fn_ref[...] = jnp.where(row8 == 3, 1.0, 0.0)

    def features(values, first_leaf, put):
        x = ((values[0] - first_leaf.astype(F32)) - 0.5) * SCALE
        y, z = (values[1] - 0.5) * SCALE, (values[2] - 0.5) * SCALE
        moved = x + SCALE
        flat = y * y + z * z
        for j, value in enumerate((x, y, z, x * x + flat)):
            put(fa_ref, j, value)
        for ref, along in ((fs_ref, x), (fn_ref, moved)):
            for j, value in ((0, -2.0 * along), (1, -2.0 * y), (2, -2.0 * z), (4, along * along + flat + soft)):
                put(ref, j, value)

    def put_own(ref, j, value):
        ref[pl.ds(8 + j, PART, stride=8), :] = value

    def put_left(ref, j, value):
        ref[j : j + 1, :] = value

    def put_right(ref, j, value):
        at = (PART + 1) * 8 + j
        ref[at : at + 1, :] = value

    features([pt_ref[0], pt_ref[1], pt_ref[2]], iota((PART, LANES), 0) + base, put_own)
    one_leaf = iota((1, LANES), 0) + base
    features(left, one_leaf - 1, put_left)
    features(right, one_leaf + PART, put_right)

    def lists(i, offset):
        wanted = base + i + offset
        at = first_leaf + i
        hit = (list_ref[0, at] == wanted) | (list_ref[1, at] == wanted) | (list_ref[2, at] == wanted)
        return jnp.where(hit, 1.0, 0.0).astype(F32)

    def pieces(ref, w):
        return three(ref[pl.ds(pl.multiple_of(w * 8, 8), 8), :])

    def source_of(w):
        a, b, c = pieces(fa_ref, w)
        return jnp.concatenate([a, a, b, b, a, c], axis=0).astype(BF16)

    def target_of(ref, w):
        a, b, c = pieces(ref, w)
        return jnp.concatenate([a, b, a, b, c, a], axis=0).astype(BF16)

    def kernel_of(source, target):
        return lax.rsqrt(dot_tn(source, target)).astype(BF16)

    first = dot(left_charges, kernel_of(source_of(0), target_of(fn_ref, 1)))

    def fill(i, carry):
        both = jnp.concatenate([target_of(fs_ref, i + 1), target_of(fn_ref, i + 2)], axis=1)
        k_ref[i] = kernel_of(source_of(i + 1), both)
        return carry


    def step(i, carry, own, after):
        spread = dot(own, k_ref[i])
        back = dot_nt(after, k_ref[i, :, LANES : 2 * LANES])
        out_ref[i] = carry + spread[:, 0:LANES] + lists(i, 1) * back
        return spread[:, LANES : 2 * LANES]

    def body(i, carry):
        onward = step(i, carry, ch_ref[i], ch_ref[i + 1])
        return lists(i + 1, -1) * onward

    carry = lists(0, -1) * first
    for i in range(AHEAD):
        fill(i, 0)
    for i in range(PART - 1):
        if i + AHEAD < PART:
            fill(i + AHEAD, 0)
        carry = body(i, carry)
    step(PART - 1, carry, ch_ref[PART - 1], right_charges)


VMEM = pl.BlockSpec(memory_space=pltpu.VMEM)
SMEM = pl.BlockSpec(memory_space=pltpu.SMEM)
ANY = pl.BlockSpec(memory_space=pl.ANY)


def scratch(*shape, dtype=F32):
    return pltpu.VMEM(shape, dtype)


def shape(*dims):
    return jax.ShapeDtypeStruct(dims, F32)


def whole(*dims):
    return pl.BlockSpec(dims, lambda i, par: (0,) * len(dims))


NEAR_SCRATCH = [scratch(FRAME, LANES)] * 3 + [scratch(PART, LANES, 2 * LANES, dtype=BF16)]
FOUR = pl.BlockSpec((8, 1024), lambda i, par: (par[0] >> 1, 0))
TWO = pl.BlockSpec((8, 1024), lambda i, par: (64 + (par[0] >> 2), 0))
LEAF_SPEC = pl.BlockSpec((HEAD, LANES), lambda i, par: (0, 0))
FOUR_C = pl.BlockSpec((3, 8, 1024), lambda i, par: (0, par[0] >> 1, 0))
TWO_C = pl.BlockSpec((3, 8, 1024), lambda i, par: (0, 64 + (par[0] >> 2), 0))


def call(kernel, in_specs, out_specs, out_shape, scratch_shapes):
    return pl.pallas_call(
        kernel,
        grid_spec=pltpu.PrefetchScalarGridSpec(
            num_scalar_prefetch=1,
            grid=(1,),
            in_specs=in_specs,
            out_specs=out_specs,
            scratch_shapes=scratch_shapes,
        ),
        out_shape=out_shape,
    )


def hop_partner(device, bit):
    if bit == 0 or bit & 1:
        return device ^ (1 << bit)
    low = bit - 1
    place = (device >> low) & 3
    other = (place + 1) & 3 if place & 1 else (place - 1) & 3
    return device + ((other - place) << low)


def on_device(
    charges, points, basis, near_list, loc_coupling, loc_transfer, loc_lists, top_coupling, top_transfer, top_lists
):
    devices = lax.axis_size("cluster")
    d = lax.axis_index("cluster")
    mates = [(i, i ^ 1) for i in range(devices)]
    others = [(i, ((i + 1) ^ 1) - 1) for i in range(devices) if 0 <= ((i + 1) ^ 1) - 1 < devices]
    par = d.astype(jnp.int32).reshape(1)
    points_t = jnp.transpose(points, (1, 0, 2))
    transfer = loc_transfer[0]
    coupling = jnp.transpose(loc_coupling[0], (1, 0, 2))
    top_c = jnp.transpose(top_coupling, (1, 0, 2))
    top_l = jnp.transpose(top_lists)
    message = HEAD + ROWS[0]
    moments, msg_near, msg_far, device_moment = call(
        up_kernel,
        [whole(LANES, NK, LANES), whole(3, LANES, LANES), ANY, ANY, FOUR, TWO],
        [whole(M_ROWS, LANES), whole(message, LANES), whole(message, LANES), whole(1, 512)],
        [shape(M_ROWS, LANES), shape(message, LANES), shape(message, LANES), shape(1, 512)],
        [
            scratch(2048, LANES),
            scratch(512, LANES),
            scratch(1024, LANES, dtype=BF16),
            scratch(1024, LANES),
            scratch(LANES, RANK, LANES, dtype=BF16),
            scratch(248, 1024, dtype=BF16),
            pltpu.SemaphoreType.DMA((PARTS + 1,)),
        ],
    )(par, charges, points_t, basis, transfer, top_transfer, top_transfer)

    halo_near = lax.ppermute(msg_near, "cluster", mates)
    halo_far = lax.ppermute(msg_far, "cluster", others)
    gathered = device_moment
    for bit in range(7):
        partner = lax.ppermute(gathered, "cluster", [(i, hop_partner(i, bit)) for i in range(devices)])
        if bit == 6:
            break
        upper = ((d >> bit) & 1) == 1
        gathered = jnp.concatenate(
            [jnp.where(upper, partner, gathered), jnp.where(upper, gathered, partner)], axis=0
        )

    near_list_t = near_list.T
    near = []
    for part in range(PARTS):
        lower, upper_leaf = max(PART * part - 1, 0), min(PART * (part + 1), LANES - 1)
        specs = [
            SMEM,
            pl.BlockSpec((3, PART, LANES), lambda i, par, p=part: (0, p, 0)),
            pl.BlockSpec((PART, NK, LANES), lambda i, par, p=part: (p, 0, 0)),
            pl.BlockSpec((3, 8, LANES), lambda i, par, p=lower: (0, p // 8, 0)),
            pl.BlockSpec((1, NK, LANES), lambda i, par, p=lower: (p, 0, 0)),
            pl.BlockSpec((3, 8, LANES), lambda i, par, p=upper_leaf: (0, p // 8, 0)),
            pl.BlockSpec((1, NK, LANES), lambda i, par, p=upper_leaf: (p, 0, 0)),
        ]
        operands = [near_list_t, points_t, charges, points_t, charges, points_t, charges]
        if part in (0, PARTS - 1):
            specs += [LEAF_SPEC, LEAF_SPEC]
            operands += [halo_near, halo_far]
        near.append(
            call(
                functools.partial(near_kernel, part),
                specs,
                whole(PART, NK, LANES),
                shape(PART, NK, LANES),
                NEAR_SCRATCH,
            )(par, *operands)
        )

    coupled = []
    fine_lists = jnp.transpose(loc_lists, (2, 0, 1))
    for levels in ((0,), (1, 2, 3, 4, 5)):
        out_rows = sum(ROWS[level] for level in levels)
        coupled.append(
            call(
                functools.partial(couple_kernel, levels),
                [
                    pl.BlockSpec((ROWS[0], LANES), lambda i, par, t=levels[0]: (t, 0)),
                    whole(HEAD + ROWS[levels[0]], LANES),
                    whole(HEAD + ROWS[levels[0]], LANES),
                    whole(3, 1, 248),
                    SMEM,
                    pl.BlockSpec((3, LANES, 1024), lambda i, par, t=min(levels[0], 1): (0, t, 0)),
                    FOUR_C,
                    TWO_C,
                ],
                whole(out_rows, LANES),
                shape(out_rows, LANES),
                [scratch(1536, LANES), scratch(3072, LANES, dtype=BF16), scratch(3072, LANES), scratch(8, 2 * LANES)],
            )(par, moments, halo_near, halo_far, fine_lists, top_l, coupling, top_c, top_c)
        )

    return call(
        finish_kernel,
        [
            SMEM,
            whole(LANES // 2, 512),
            whole(LANES // 2, 512),
            pl.BlockSpec((256, 1024), lambda i, par: (3, 0)),
        ]
        + [
            pl.BlockSpec((3, 8, 1024), lambda i, par, t=level: (0, 128 - (32 >> t) + (par[0] >> (t + 3)), 0))
            for level in range(6)
        ]
        + [
            FOUR,
            TWO,
        ]
        + [ANY] * (4 + PARTS),
        ANY,
        shape(LANES, NK, LANES),
        [
            scratch(512, LANES),
            scratch(START[6], LANES),
            scratch(512, LANES),
            scratch(1024, LANES, dtype=BF16),
            scratch(1024, LANES),
            scratch(96, LANES),
            scratch(3072, LANES),
            scratch(1024, LANES),
            scratch(512, LANES),
            scratch(512, LANES),
            scratch(2048, LANES),
            scratch(1024, LANES),
            scratch(248, 1024, dtype=BF16),
            scratch(ROWS[0], LANES),
            scratch(M_ROWS - ROWS[0], LANES),
            scratch(LANES, RANK, LANES, dtype=BF16),
            scratch(LANES, NK, LANES),
            scratch(LANES, NK, LANES),
            pltpu.SemaphoreType.DMA((8 + PARTS,)),
        ],
    )(par, top_l, gathered, partner, top_transfer, *([top_c] * 6), top_transfer, top_transfer, transfer, *coupled, basis, *near)


def solution(mesh):
    placed = (
        P("cluster", None, None),
        P("cluster", None, None),
        P("cluster", None, None),
        P("cluster", None),
        P("cluster", None, None, None),
        P("cluster", None, None),
        P("cluster", None, None),
        P(),
        P(),
        P(),
    )
    return jax.shard_map(on_device, mesh=mesh, in_specs=placed, out_specs=P("cluster", None, None), check_vma=False)
```
